32 devices in a mesh: sub: 8 (over y, x, core), grp: 4 (over z).
Axes of the slice: x: 2, y: 2, z: 4, core: 2. Of those that a mesh axis runs over, the one named last changes fastest.
Arguments:
- node_rows: bfloat16 [32768, 512], P(('sub', 'grp')), may hold values from -6 to 6
- owners: int32 [32768], P(('sub', 'grp')), may hold values from 0 to 31, as said below
- tile_src: int32 [8, 4, 16, 2], P('sub', 'grp'), may hold values from 0 to 15
- neighbors: int32 [8, 4, 2048, 16], P('sub', 'grp'), may hold values from 0 to 127
- pool_pair: int32 [8, 4, 2048], P('sub', 'grp'), may hold values from 0 to 2047, each once within a row
- pool_quad: int32 [4, 4, 2048], P(None, 'grp'), may hold values from 0 to 2047, each once within a row
- pool_top: int32 [2, 4, 2048], P(None, 'grp'), may hold values from 0 to 2047, each once within a row
- edge_in: bfloat16 [2, 512, 512], replicated, may hold values from -0.25 to 0.25
- edge_bias: float32 [512], replicated, may hold values from -4 to 4
- edge_out: bfloat16 [512, 512], replicated, may hold values from -0.25 to 0.25
- node_in: bfloat16 [2, 512, 512], replicated, may hold values from -0.25 to 0.25
- node_bias: float32 [512], replicated, may hold values from -4 to 4
- node_out: bfloat16 [512, 512], replicated, may hold values from -0.25 to 0.25
- out_gain: float32 [512], replicated, may hold values from 0.1 to 1.9
- coarse: bfloat16 [3, 512, 512], replicated, may hold values from -0.25 to 0.25
Outputs:
- updated: bfloat16 [65536, 512], P(('sub', 'grp'))
The draws below stay inside these ranges and needn't reach their ends.
Inputs may be any that keep to these rules, and one draw needn't show every extreme that they name: `owners`: at most 64 nodes of one shard go to one owner, and one owner receives exactly 64 nodes from every shard. `pool_pair`: every row of the pooling map is a permutation of the 2048 slots. `pool_quad`: every row of the pooling map is a permutation of the 2048 slots. `pool_top`: every row of the pooling map is a permutation of the 2048 slots.
All inputs are finite; a program needn't handle non-finite values.
Results may differ from the reference program's by a relative error of at most 0.007.
Values may be sent and summed in bfloat16 or wider, within the bound.
A program may use at most 64 MiB of HBM per device.

```python
import jax
import jax.numpy as jnp
from jax import lax

W = 512
OWN_DEV = 2048
BLK = 128
TPB = 2
NBR = 8
OWNERS = 32
CAP = 64
NODE_DEV = 1024
NODES = 32768
BLOCKS = 16
N_SUB = 8
N_GRP = 4


def draw_owners(key, part):
    favored = jax.random.randint(jax.random.fold_in(key, 7), (), 0, OWNERS).astype(jnp.int32)
    slot_total = OWNERS * CAP

    def one_source(source):
        source_key = jax.random.fold_in(key, source + 11)
        shuffled = jax.random.permutation(jax.random.fold_in(source_key, 1), slot_total).astype(jnp.int32)
        owner_of = shuffled // CAP
        ranking = jnp.arange(slot_total, dtype=jnp.int32) + slot_total * (owner_of == favored).astype(jnp.int32)
        picked = owner_of[jnp.argsort(ranking, stable=True)[:NODE_DEV - CAP]]
        listing = jnp.concatenate([jnp.full((CAP,), favored, jnp.int32), picked.astype(jnp.int32)])
        return jax.random.permutation(jax.random.fold_in(source_key, 2), listing)
    return jax.vmap(one_source)(jnp.arange(OWNERS, dtype=jnp.int32)).reshape(-1).astype(jnp.int32)


def touch_ends(drawn, key, smallest, high):
    place = [jax.random.randint(jax.random.fold_in(key, axis), (), 0, length) for axis, length in enumerate(drawn.shape)]
    longest = drawn.shape.index(max(drawn.shape))
    next_to = place[:longest] + [(place[longest] + 1) % drawn.shape[longest]] + place[longest + 1:]
    return drawn.at[tuple(place)].set(smallest).at[tuple(next_to)].set(high)


def steps_of(stream_key, shape, split, smallest, top_value):
    loudness, own = 1.0, jax.random.fold_in(stream_key, 6)
    for dim, blocks in split:
        heights = jnp.exp(jax.random.uniform(jax.random.fold_in(own, dim), (blocks,), jnp.float32, smallest / len(split), top_value / len(split)))
        loudness = loudness * jnp.repeat(heights, shape[dim] // blocks).reshape([-1 if axis == dim else 1 for axis in range(len(shape))])
    return loudness


def normal_values(own_key, shape, width, bound, shards=(), kind=jnp.bfloat16):
    level = steps_of(own_key, shape, shards, -0.22, 0.18) if shards else 1.0
    array = jax.random.normal(own_key, shape, jnp.float32) * width * level
    return jnp.minimum(jnp.maximum(array, -bound), bound).astype(kind)


def setup_inputs(seed: int = 0) -> dict:
    streams_of = jax.random.split(jax.random.key(seed), 16)
    node_rows = normal_values(streams_of[0], (NODES, W), 1.0, 6.0, ((0, 32),))
    owners = draw_owners(jax.random.fold_in(streams_of[15], 71), 0)
    tile_src = touch_ends(jax.random.randint(streams_of[2], (N_SUB, N_GRP, BLOCKS, TPB), 0, BLOCKS), jax.random.fold_in(streams_of[2], 1), 0, BLOCKS - 1).astype(jnp.int32)
    neighbors = touch_ends(jax.random.randint(streams_of[3], (N_SUB, N_GRP, OWN_DEV, TPB * NBR), 0, BLK), jax.random.fold_in(streams_of[3], 1), 0, BLK - 1).astype(jnp.int32)
    pool_pair = jax.vmap(lambda own: jax.random.permutation(own, OWN_DEV))(jax.random.split(streams_of[4], N_SUB * N_GRP)).reshape((N_SUB, N_GRP, OWN_DEV)).astype(jnp.int32)
    pool_quad = jax.vmap(lambda own: jax.random.permutation(own, OWN_DEV))(jax.random.split(streams_of[5], (N_SUB // 2) * N_GRP)).reshape((N_SUB // 2, N_GRP, OWN_DEV)).astype(jnp.int32)
    pool_top = jax.vmap(lambda own: jax.random.permutation(own, OWN_DEV))(jax.random.split(streams_of[6], (N_SUB // 4) * N_GRP)).reshape((N_SUB // 4, N_GRP, OWN_DEV)).astype(jnp.int32)
    edge_in = normal_values(streams_of[7], (2, W, W), W ** -0.5, 0.25)
    edge_bias = normal_values(streams_of[8], (W,), 1.0, 4.0, (), jnp.float32)
    edge_out = normal_values(streams_of[9], (W, W), W ** -0.5, 0.25)
    node_in = normal_values(streams_of[10], (2, W, W), W ** -0.5, 0.25)
    node_bias = normal_values(streams_of[11], (W,), 1.0, 4.0, (), jnp.float32)
    node_out = normal_values(streams_of[12], (W, W), W ** -0.5, 0.25)
    out_gain = jnp.clip(1.0 + 0.18 * jax.random.normal(streams_of[13], (W,), jnp.float32), 0.1, 1.9)
    coarse = normal_values(streams_of[14], (3, W, W), W ** -0.5, 0.25)
    return dict(node_rows=node_rows, owners=owners, tile_src=tile_src, neighbors=neighbors, pool_pair=pool_pair, pool_quad=pool_quad, pool_top=pool_top, edge_in=edge_in, edge_bias=edge_bias, edge_out=edge_out, node_in=node_in, node_bias=node_bias, node_out=node_out, out_gain=out_gain, coarse=coarse)


epsilon = 1e-05

def place_slots(node_rows, owners):
    source_owner = owners.reshape(OWNERS, NODE_DEV)
    matches = (source_owner[:, :, None] == jnp.arange(OWNERS, dtype=jnp.int32)[None, None, :]).astype(jnp.int32)
    position = lax.optimization_barrier(jnp.sum((jnp.cumsum(matches, axis=1) - matches) * matches, axis=2))
    source_index = jnp.arange(OWNERS, dtype=jnp.int32)[:, None]
    target = (source_owner * OWN_DEV + source_index * CAP + position).reshape(-1).astype(jnp.int32)
    slots = jnp.zeros((OWNERS * OWN_DEV, W), jnp.bfloat16).at[target].set(node_rows)
    present = jnp.zeros((OWNERS * OWN_DEV,), jnp.float32).at[target].set(1.0)
    return (slots.reshape(OWNERS, OWN_DEV, W), present.reshape(OWNERS, OWN_DEV))

def block_sum(proj_dst, proj_src, present, tile_rows, near_rows, block_index):
    start = block_index * BLK
    dst_rows = lax.dynamic_slice_in_dim(proj_dst, start, BLK, 0).astype(jnp.float32)
    near_block = lax.dynamic_slice_in_dim(near_rows, start, BLK, 0)
    base = jnp.repeat(tile_rows[block_index], NBR) * BLK
    source = (base[None, :] + near_block).astype(jnp.int32)
    gathered = proj_src[source].astype(jnp.float32)
    weight = present[source]
    return lax.optimization_barrier(jnp.sum(jax.nn.silu(dst_rows[:, None, :] + gathered) * weight[:, :, None], axis=1))

def fine_update(slots, present, tile_rows, near_rows, edge_in, edge_bias, edge_out, node_in, node_bias, node_out, out_gain):
    proj_dst = (jnp.dot(slots, edge_in[0], preferred_element_type=jnp.float32) + edge_bias).astype(jnp.bfloat16)
    proj_src = jnp.dot(slots, edge_in[1], preferred_element_type=jnp.float32).astype(jnp.bfloat16)
    summed = lax.map(lambda block_index: block_sum(proj_dst, proj_src, present, tile_rows, near_rows, block_index), jnp.arange(BLOCKS, dtype=jnp.int32))
    agg = summed.reshape(OWN_DEV, W).astype(jnp.bfloat16)
    message = jnp.dot(agg, edge_out, preferred_element_type=jnp.float32).astype(jnp.bfloat16)
    hidden = jax.nn.silu(jnp.dot(slots, node_in[0], preferred_element_type=jnp.float32) + jnp.dot(message, node_in[1], preferred_element_type=jnp.float32) + node_bias).astype(jnp.bfloat16)
    delta = jnp.dot(hidden, node_out, preferred_element_type=jnp.float32)
    normed = delta * lax.rsqrt(lax.optimization_barrier(jnp.mean(delta * delta, axis=-1, keepdims=True)) + epsilon)
    return (present[:, None] * (slots.astype(jnp.float32) + out_gain * normed)).astype(jnp.bfloat16)

def refine(total, count, weight):
    mean_rows = total / jnp.maximum(count, 1.0)[..., None]
    rounded = mean_rows.astype(jnp.bfloat16)
    lifted = jnp.dot(rounded.reshape(-1, W), weight, preferred_element_type=jnp.float32).reshape(mean_rows.shape)
    return (mean_rows + jax.nn.silu(lifted)).astype(jnp.bfloat16)

def invert(perm):
    flat = perm.reshape(-1, OWN_DEV)
    inverse = jax.vmap(lambda single: jnp.zeros((OWN_DEV,), jnp.int32).at[single].set(jnp.arange(OWN_DEV, dtype=jnp.int32)))(flat)
    return inverse.reshape(perm.shape)

def pick_rows(values, perm):
    return jnp.take_along_axis(values, perm[..., None], axis=-2)

def reference(node_rows, owners, tile_src, neighbors, pool_pair, pool_quad, pool_top, edge_in, edge_bias, edge_out, node_in, node_bias, node_out, out_gain, coarse):
    slots, present = place_slots(node_rows, owners)
    tiles = tile_src.reshape(OWNERS, BLOCKS, TPB)
    nears = neighbors.reshape(OWNERS, OWN_DEV, TPB * NBR)
    fine = lax.map(lambda packed: fine_update(packed[0], packed[1], packed[2], packed[3], edge_in, edge_bias, edge_out, node_in, node_bias, node_out, out_gain), (slots, present, tiles, nears))
    fine4 = fine.reshape(N_SUB, N_GRP, OWN_DEV, W)
    present4 = present.reshape(N_SUB, N_GRP, OWN_DEV)
    count_side = jnp.take_along_axis(present4, pool_pair, axis=2)
    term = (count_side[..., None] * pick_rows(fine4, pool_pair).astype(jnp.float32)).reshape(N_SUB // 2, 2, N_GRP, OWN_DEV, W)
    counts = count_side.reshape(N_SUB // 2, 2, N_GRP, OWN_DEV)
    count1 = counts[:, 0] + counts[:, 1]
    level1 = refine(term[:, 0] + term[:, 1], count1, coarse[0])
    count_side = jnp.take_along_axis(count1, pool_quad, axis=2)
    term = (count_side[..., None] * pick_rows(level1, pool_quad).astype(jnp.float32)).reshape(N_SUB // 4, 2, N_GRP, OWN_DEV, W)
    counts = count_side.reshape(N_SUB // 4, 2, N_GRP, OWN_DEV)
    count2 = counts[:, 0] + counts[:, 1]
    level2 = refine(term[:, 0] + term[:, 1], count2, coarse[1])
    count_side = jnp.take_along_axis(count2, pool_top, axis=2)
    term = count_side[..., None] * pick_rows(level2, pool_top).astype(jnp.float32)
    level3 = refine(lax.optimization_barrier(jnp.sum(term, axis=1)), lax.optimization_barrier(jnp.sum(count_side, axis=1)), coarse[2])
    spread3 = jnp.broadcast_to(level3[:, None], (N_SUB // 4, N_GRP, OWN_DEV, W))
    back2 = (level2.astype(jnp.float32) + pick_rows(spread3, invert(pool_top)).astype(jnp.float32)).astype(jnp.bfloat16)
    back1 = (level1.astype(jnp.float32) + pick_rows(jnp.repeat(back2, 2, axis=0), invert(pool_quad)).astype(jnp.float32)).astype(jnp.bfloat16)
    lifted = pick_rows(jnp.repeat(back1, 2, axis=0), invert(pool_pair)).astype(jnp.float32)
    updated = present4[..., None] * (fine4.astype(jnp.float32) + lifted)
    return updated.reshape(OWNERS * OWN_DEV, W).astype(jnp.bfloat16)
```

```python
import functools

import jax
import jax.numpy as jnp
from jax import lax
from jax.experimental import pallas as pl
from jax.experimental.pallas import tpu as pltpu
from jax.sharding import PartitionSpec as P

BLK = 128
TPB = 2
NBR = 8
LANES = 128
PAD = 16
EMPTY = 16384.0
LIMIT = 8192.0
AWAY = -8192.0
epsilon = 1e-05
f32 = jnp.float32
bf16 = jnp.bfloat16

VM = pl.BlockSpec(memory_space=pltpu.VMEM)
SM = pl.BlockSpec(memory_space=pltpu.SMEM)


def call(kernel, outs, args, specs=None, scratch=(), flops=0):
    return pl.pallas_call(
        kernel,
        out_shape=outs,
        in_specs=specs or [VM] * len(args),
        out_specs=jax.tree.map(lambda _: VM, outs),
        scratch_shapes=list(scratch),
        compiler_params=pltpu.CompilerParams(vmem_limit_bytes=44 << 20),
        cost_estimate=pl.CostEstimate(flops=flops, bytes_accessed=8 << 20, transcendentals=0),
    )(*args)


def rows_of(shape, start=0):
    return lax.broadcasted_iota(jnp.int32, shape, 0) + start


def lanes_of(shape, start=0):
    return lax.broadcasted_iota(jnp.int32, shape, 1) + start


def one_hot(mask):
    return jnp.where(mask, 1.0, 0.0).astype(bf16)


def spread(row):
    return jnp.broadcast_to(row, (LANES, LANES)).T


def dot(a, b):
    return jnp.dot(a, b, preferred_element_type=f32)


def half_silu(h):
    return h + h * jnp.tanh(h)


def picker(perm_ref, first, count, start, width):
    tiles = []
    for c in range(0, count, LANES):
        column = spread(perm_ref[:, pl.ds(pl.multiple_of(first + c, LANES), LANES)])
        wide = jnp.concatenate([column] * (width // LANES), axis=1)
        tiles.append(one_hot(wide == lanes_of((LANES, width), start)))
    return jnp.concatenate(tiles, axis=0)


def place_kernel(cap, owners_ref, nodes_ref, out_ref):
    owner_row = owners_ref[...]
    nodes = owner_row.shape[1]
    position = jnp.zeros((1, nodes), f32)
    for c in range(0, nodes, LANES):
        column = spread(owners_ref[:, c : c + LANES])
        wide = jnp.concatenate([column] * (nodes // LANES), axis=1)
        shape = (LANES, nodes)
        earlier = (wide == owner_row) & (rows_of(shape, c) < lanes_of(shape))
        position += jnp.sum(jnp.where(earlier, 1.0, 0.0), axis=0, keepdims=True)
    target = owner_row * cap + position.astype(jnp.int32)
    tile = 256

    @pl.loop(0, out_ref.shape[0] // tile)
    def _(t):
        start = pl.multiple_of(t * tile, tile)
        mask = rows_of((tile, nodes), start) == target
        weight = jnp.where(mask, 1.0, 0.0)
        filled = jnp.max(weight, axis=1, keepdims=True)
        rows = dot(weight.astype(bf16), nodes_ref[...])
        out_ref[pl.ds(start, tile), :] = jnp.where(filled > 0.5, rows, EMPTY).astype(bf16)


def compose_kernel(pair_ref, quad_ref, top_ref, two_ref, three_ref, parts, sums):
    width = pair_ref.shape[1]
    tile = 256

    def compose(outer, inner_row, out_ref):
        which = rows_of((8, width))
        high = (outer >> 7).astype(f32)
        low = (outer & 127).astype(f32)
        parts[...] = jnp.where(which == 0, high, jnp.where(which == 1, low, 0.0))
        sums[...] = jnp.zeros_like(sums)

        @pl.loop(0, width // tile)
        def _(t):
            start = pl.multiple_of(t * tile, tile)
            sel = one_hot(rows_of((tile, width), start) == inner_row)
            sums[...] += dot(parts[:, pl.ds(start, tile)].astype(bf16), sel)

        total = sums[...]
        out_ref[...] = (total[0:1] * 128.0 + total[1:2]).astype(jnp.int32)

    compose(pair_ref[...], quad_ref[...], two_ref)
    compose(two_ref[...], top_ref[...], three_ref)


def fine_kernel(
    tile_ref,
    arrived_ref,
    near_ref,
    edge_in_ref,
    edge_bias_ref,
    edge_out_ref,
    node_in_ref,
    node_bias_ref,
    node_out_ref,
    gain_ref,
    fine_ref,
    slots,
    dst,
    src,
    agg,
    sels,
    near_rows,
):
    count, features = fine_ref.shape
    tile = 256

    @pl.loop(0, count // tile)
    def _(t):
        here = pl.ds(pl.multiple_of(t * tile, tile), tile)
        raw = arrived_ref[here, :].astype(f32)
        present = raw[:, 0:1] < LIMIT
        rows = jnp.where(present, raw, 0.0).astype(bf16)
        slots[here, :] = rows
        to_dst = (dot(rows, edge_in_ref[0]) + edge_bias_ref[...]) * 0.5
        dst[here, :] = to_dst.astype(bf16)
        from_src = dot(rows, edge_in_ref[1]) * 0.5
        src[here, :] = jnp.where(present, from_src, AWAY).astype(bf16)

    group = 16

    @pl.loop(0, count // BLK)
    def _(b):
        start = pl.multiple_of(b * BLK, BLK)
        near = near_ref[pl.ds(start, BLK), :]
        for j in range(TPB):
            for k in range(NBR):
                at = j * NBR + k
                mask = near[:, at : at + 1] == lanes_of((BLK, BLK))
                sels[k * BLK : (k + 1) * BLK, :] = one_hot(mask)
            first = pl.multiple_of(tile_ref[b, j] * BLK, BLK)
            near_rows[j * NBR * BLK : (j + 1) * NBR * BLK, :] = dot(
                sels[...], src[pl.ds(first, BLK), :]
            )
        for r in range(0, BLK, group):
            here = dst[pl.ds(start + r, group), :].astype(f32)
            total = jnp.zeros((group, features), f32)
            for at in range(TPB * NBR):
                total += half_silu(here + near_rows[at * BLK + r : at * BLK + r + group, :])
            agg[pl.ds(start + r, group), :] = total.astype(bf16)

    @pl.loop(0, count // tile)
    def _(t):
        here = pl.ds(pl.multiple_of(t * tile, tile), tile)
        rows = slots[here, :]
        message = dot(agg[here, :], edge_out_ref[...]).astype(bf16)
        lifted = dot(rows, node_in_ref[0]) + dot(message, node_in_ref[1]) + node_bias_ref[...]
        hidden = half_silu(lifted * 0.5).astype(bf16)
        delta = dot(hidden, node_out_ref[...])
        scale = lax.rsqrt(jnp.mean(delta * delta, axis=-1, keepdims=True) + epsilon)
        fine = rows.astype(f32) + gain_ref[...] * (delta * scale)
        present = arrived_ref[here, 0:LANES].astype(f32)[:, 0:1] < LIMIT
        fine_ref[here, :] = jnp.where(present, fine, EMPTY).astype(bf16)


def refined(total, count, weight):
    mean_rows = total * (1.0 / jnp.maximum(count, 1.0))
    lifted = dot(mean_rows.astype(bf16), weight)
    return mean_rows + half_silu(lifted * 0.5)


def widened(column, features):
    return jnp.concatenate([column] * (features // LANES), axis=1)


def put_counts(out_ref, rows, columns):
    features = out_ref.shape[1]
    parts = [col.T[0:1, :] for col in columns]
    parts += [jnp.zeros((1, LANES), f32)] * (features // LANES - len(parts))
    line = jnp.concatenate(parts, axis=1)
    tail = jnp.where(rows_of((PAD, features)) == 0, line, 0.0)
    out_ref[pl.ds(rows, PAD), :] = tail.astype(bf16)


def get_count(tail, c):
    return spread(tail[0:1, c : c + LANES])


def tree_kernel(
    groups,
    fine_ref,
    pair_ref,
    quad_ref,
    top_ref,
    two_ref,
    three_ref,
    coarse_ref,
    out_ref,
    side,
    partner,
    level_one,
    wide_one,
    mine,
    theirs,
    wide_two,
    packets,
    inbox,
    level_three,
    raised,
    side_sems,
    quad_sems,
    two_sems,
    group_sems,
    spread_sems,
):
    count, features = fine_ref.shape
    half = quad_ref.shape[1]
    quarter = top_ref.shape[1]
    piece = quarter // groups
    packet = piece + PAD
    tile = 256
    a, g = lax.axis_index("sub"), lax.axis_index("grp")
    core = a + 1 - 2 * (a % 2)
    across = a + 2 - 4 * ((a // 2) % 2)
    others = [lax.rem(g + d, groups) for d in range(1, groups)]
    peers = [{"grp": t} for t in others] + [{"sub": across}, {"sub": core}]
    barrier = pltpu.get_barrier_semaphore()
    for peer in peers:
        pl.semaphore_signal(barrier, inc=1, device_id=peer, device_id_type=pl.DeviceIdType.MESH)
    pl.semaphore_wait(barrier, len(peers))

    def send(sems, at, source, target, peer):
        copy = pltpu.make_async_remote_copy(
            src_ref=source,
            dst_ref=target,
            send_sem=sems.at[(0, *at)],
            recv_sem=sems.at[(1, *at)],
            device_id=peer,
            device_id_type=pl.DeviceIdType.MESH,
        )
        copy.start()
        return copy

    many = 512
    sides = []
    for t in range(count // many):
        here = pl.ds(t * many, many)
        sel = picker(pair_ref, t * many, many, 0, count)
        side[here, :] = dot(sel, fine_ref[...]).astype(bf16)
        sides.append(send(side_sems, (t,), side.at[here, :], partner.at[here, :], {"sub": core}))
    for t in range(count // many):
        sides[t].wait_recv()
        for start in range(t * many, (t + 1) * many, tile):
            here = pl.ds(start, tile)
            x = side[here, :].astype(f32)
            y = partner[here, :].astype(f32)
            in_x = x[:, 0:1] < LIMIT
            in_y = y[:, 0:1] < LIMIT
            total = jnp.where(in_x, x, 0.0) + jnp.where(in_y, y, 0.0)
            marks = jnp.where(in_x, 1.0, 0.0) + jnp.where(in_y, 1.0, 0.0)
            level = refined(total, marks, coarse_ref[0]).astype(bf16)
            level_one[here, :] = level
            wide_one[here, 0:features] = level
            wide_one[here, features : features + LANES] = jnp.broadcast_to(
                marks, (tile, LANES)
            ).astype(bf16)

    block = tile + PAD
    quads = []
    for t in range(half // tile):
        sel = picker(quad_ref, t * tile, tile, 0, count)
        got = dot(sel, wide_one[...])
        mine[t * block : t * block + tile, :] = got[:, 0:features].astype(bf16)
        columns = [got[c : c + LANES, features : features + LANES] for c in range(0, tile, LANES)]
        put_counts(mine, t * block + tile, columns)
        here = pl.ds(t * block, block)
        quads.append(send(quad_sems, (t,), mine.at[here, :], theirs.at[here, :], {"sub": across}))

    @pl.loop(0, count // tile)
    def _(t):
        start = pl.multiple_of(t * tile, tile)
        here = pl.ds(start, tile)
        sel = one_hot(rows_of((tile, count), start) == pair_ref[...])
        raised[here, :] = fine_ref[here, :].astype(f32) + dot(sel, level_one[...])

    base = pl.multiple_of((a % 2) * half, half)
    twos = []
    for t in range(half // tile):
        quads[t].wait_recv()
        my_tail = mine[t * block + tile : (t + 1) * block, :].astype(f32)
        their_tail = theirs[t * block + tile : (t + 1) * block, :].astype(f32)
        for c in range(0, tile, LANES):
            x, y = get_count(my_tail, c), get_count(their_tail, c)
            at = t * block + c
            total = widened(x, features) * mine[at : at + LANES, :].astype(f32) + widened(
                y, features
            ) * theirs[at : at + LANES, :].astype(f32)
            level = refined(total, widened(x + y, features), coarse_ref[1])
            there = pl.ds(base + t * tile + c, LANES)
            wide_two[there, 0:features] = level.astype(bf16)
            wide_two[there, features : features + LANES] = (x + y).astype(bf16)
        there = wide_two.at[pl.ds(base + t * tile, tile), :]
        twos.append(send(two_sems, (t,), there, there, {"sub": core}))
    for copy in twos:
        copy.wait_recv()

    sel = picker(top_ref, 0, quarter, 0, count)
    got = dot(sel, wide_two[...])
    for t in range(groups):
        at, first = t * packet, t * piece
        packets[at : at + piece, :] = got[first : first + piece, 0:features].astype(bf16)
        columns = [
            got[first + c : first + c + LANES, features : features + LANES]
            for c in range(0, piece, LANES)
        ]
        put_counts(packets, at + piece, columns)
    parcels = []
    for d, t in enumerate(others):
        here = pl.ds(pl.multiple_of(t * packet, PAD), packet)
        parcels.append(
            send(group_sems, (d,), packets.at[here, :], inbox.at[d], {"grp": t})
        )

    @pl.loop(0, count // tile)
    def _(t):
        start = pl.multiple_of(t * tile, tile)
        here = pl.ds(start, tile)
        sel = one_hot(rows_of((tile, count), start) == two_ref[...])
        raised[here, :] += dot(sel, wide_two[:, 0:features])

    for copy in parcels:
        copy.wait_recv()
    own = pl.multiple_of(g * packet, PAD)
    terms = [lambda at, size: packets[pl.ds(own + at, size), :].astype(f32)]
    for d in range(groups - 1):
        terms.append(lambda at, size, d=d: inbox[d, at : at + size, :].astype(f32))
    tails = [term(piece, PAD) for term in terms]
    base_three = pl.multiple_of(((a % 4) * groups + g) * piece, piece)
    for c in range(0, piece, LANES):
        total, marks = 0.0, 0.0
        for term, tail in zip(terms, tails):
            got = get_count(tail, c)
            marks = marks + got
            total = total + widened(got, features) * term(c, LANES)
        level = refined(total, widened(marks, features), coarse_ref[2])
        level_three[pl.ds(base_three + c, LANES), :] = level.astype(bf16)

    def piece_of(sub, group):
        return pl.ds(pl.multiple_of(((sub % 4) * groups + group) * piece, piece), piece)

    def relay(stage, d, rows, peer):
        there = level_three.at[rows, :]
        return send(spread_sems, (stage, d), there, there, peer)

    def lift(sub, last):
        first = pl.multiple_of((sub % 4) * quarter, quarter)

        @pl.loop(0, count // tile)
        def _(t):
            start = pl.multiple_of(t * tile, tile)
            here = pl.ds(start, tile)
            sel = one_hot(rows_of((tile, quarter), start) == three_ref[:, pl.ds(first, quarter)])
            total = raised[here, :] + dot(sel, level_three[pl.ds(first, quarter), :])
            if last:
                present = fine_ref[here, 0:LANES].astype(f32)[:, 0:1] < LIMIT
                out_ref[here, :] = jnp.where(present, total, 0.0).astype(bf16)
            else:
                raised[here, :] = total

    mine_at = piece_of(a, g)
    pieces = [mine_at] + [piece_of(a, lax.rem(g + groups - d, groups)) for d in range(1, groups)]
    thence = [piece_of(across, lax.rem(g + groups - d, groups)) for d in range(groups)]
    over_x = [relay(1, 0, mine_at, {"sub": across})]
    over_z = [relay(0, d, mine_at, {"grp": t}) for d, t in enumerate(others)]
    over_core = [relay(2, 0, mine_at, {"sub": core})]
    for d in range(1, groups):
        over_z[d - 1].wait_recv()
        over_x.append(relay(1, d, pieces[d], {"sub": across}))
        over_core.append(relay(2, d, pieces[d], {"sub": core}))
    lift(a, False)
    relayed = []
    for d in range(groups):
        over_x[d].wait_recv()
        relayed.append(relay(3, d, thence[d], {"sub": core}))
    for copy in over_core:
        copy.wait_recv()
    lift(core, False)
    lift(across, False)
    for copy in relayed:
        copy.wait_recv()
    lift(across + 1 - 2 * (across % 2), True)
    for copy in sides + quads + twos + parcels + over_z + over_x + over_core + relayed:
        copy.wait_send()


def body(
    node_rows,
    owners,
    tile_src,
    neighbors,
    pool_pair,
    pool_quad,
    pool_top,
    edge_in,
    edge_bias,
    edge_out,
    node_in,
    node_bias,
    node_out,
    out_gain,
    coarse,
):
    owner_count = lax.axis_size("sub") * lax.axis_size("grp")
    slot_rows = neighbors.shape[2]
    nodes, features = node_rows.shape
    cap = slot_rows // owner_count
    me = lax.axis_index("sub")
    half, quarter = slot_rows // 2, slot_rows // 4

    def shape(rows, dtype=bf16, width=features):
        return jax.ShapeDtypeStruct((rows, width), dtype)

    placed = call(
        functools.partial(place_kernel, cap),
        shape(slot_rows),
        (owners.reshape(1, nodes), node_rows),
        flops=2 * slot_rows * nodes * features,
    )
    arrived = lax.all_to_all(
        placed.reshape(owner_count, cap, features),
        ("sub", "grp"),
        split_axis=0,
        concat_axis=0,
        tiled=True,
    ).reshape(slot_rows, features)

    pair = pool_pair.reshape(1, slot_rows)
    quad = lax.dynamic_index_in_dim(pool_quad, me // 2, 0, keepdims=False)
    top = lax.dynamic_index_in_dim(pool_top, me // 4, 0, keepdims=False)
    quad_half = lax.dynamic_slice_in_dim(quad, (me % 2) * half, half, 1)
    top_quarter = lax.dynamic_slice_in_dim(top, (me % 4) * quarter, quarter, 1)
    to_two, to_three = call(
        compose_kernel,
        (shape(1, jnp.int32, slot_rows), shape(1, jnp.int32, slot_rows)),
        (pair, quad, top),
        scratch=[pltpu.VMEM((8, slot_rows), f32), pltpu.VMEM((8, slot_rows), f32)],
        flops=20 * 10**9,
    )
    arrived, to_two, to_three = lax.optimization_barrier((arrived, to_two, to_three))

    fine = call(
        fine_kernel,
        shape(slot_rows),
        (
            tile_src[0, 0],
            arrived,
            neighbors[0, 0],
            edge_in,
            edge_bias.reshape(1, features),
            edge_out,
            node_in,
            node_bias.reshape(1, features),
            node_out,
            out_gain.reshape(1, features),
        ),
        specs=[SM] + [VM] * 9,
        scratch=[pltpu.VMEM((slot_rows, features), bf16)] * 4
        + [
            pltpu.VMEM((NBR * BLK, BLK), bf16),
            pltpu.VMEM((TPB * NBR * BLK, features), f32),
        ],
        flops=40 * 10**9,
    )
    groups = lax.axis_size("grp")
    packet = quarter // groups + PAD
    tile = 256
    rows = pltpu.VMEM((slot_rows, features), bf16)
    wide = pltpu.VMEM((slot_rows, features + LANES), bf16)
    pooled = pltpu.VMEM((half // tile * (tile + PAD), features), bf16)
    return pl.pallas_call(
        functools.partial(tree_kernel, groups),
        out_shape=shape(slot_rows),
        in_specs=[VM] * 7,
        out_specs=VM,
        scratch_shapes=[
            rows,
            rows,
            rows,
            wide,
            pooled,
            pooled,
            wide,
            pltpu.VMEM((groups * packet, features), bf16),
            pltpu.VMEM((groups - 1, packet, features), bf16),
            rows,
            pltpu.VMEM((slot_rows, features), f32),
            pltpu.SemaphoreType.DMA((2, slot_rows // 512)),
            pltpu.SemaphoreType.DMA((2, half // tile)),
            pltpu.SemaphoreType.DMA((2, half // tile)),
            pltpu.SemaphoreType.DMA((2, groups)),
            pltpu.SemaphoreType.DMA((2, 4, groups)),
        ],
        compiler_params=pltpu.CompilerParams(
            collective_id=0, has_side_effects=True, vmem_limit_bytes=48 << 20
        ),
    )(fine, pair, quad_half, top_quarter, to_two, to_three, coarse)


def solution(mesh):
    in_specs = (
        P(("sub", "grp"), None),
        P(("sub", "grp")),
        P("sub", "grp", None, None),
        P("sub", "grp", None, None),
        P("sub", "grp", None),
        P(None, "grp", None),
        P(None, "grp", None),
        P(),
        P(),
        P(),
        P(),
        P(),
        P(),
        P(),
        P(),
    )
    out_specs = P(("sub", "grp"), None)
    return jax.shard_map(body, mesh=mesh, in_specs=in_specs, out_specs=out_specs, check_vma=False)
```

```python
import functools

import jax
import jax.numpy as jnp
from jax import lax
from jax.experimental import pallas as pl
from jax.experimental.pallas import tpu as pltpu
from jax.sharding import PartitionSpec as P

BLK = 128
TPB = 2
NBR = 8
LANES = 128
PAD = 16
EMPTY = 16384.0
LIMIT = 8192.0
AWAY = -8192.0
epsilon = 1e-05
f32 = jnp.float32
bf16 = jnp.bfloat16

VM = pl.BlockSpec(memory_space=pltpu.VMEM)
SM = pl.BlockSpec(memory_space=pltpu.SMEM)
HB = pl.BlockSpec(memory_space=pltpu.HBM)


def rows_of(shape, start=0):
    return lax.broadcasted_iota(jnp.int32, shape, 0) + start


def lanes_of(shape, start=0):
    return lax.broadcasted_iota(jnp.int32, shape, 1) + start


def one_hot(mask):
    return jnp.where(mask, 1.0, 0.0).astype(bf16)


def spread(row):
    return jnp.broadcast_to(row, (LANES, LANES)).T


def dot(a, b):
    return jnp.dot(a, b, preferred_element_type=f32)


def half_silu(h):
    return h + h * jnp.tanh(h)


def picker(perm_ref, first, count, start, width):
    tiles = []
    for c in range(0, count, LANES):
        column = spread(perm_ref[:, pl.ds(pl.multiple_of(first + c, LANES), LANES)])
        wide = jnp.concatenate([column] * (width // LANES), axis=1)
        tiles.append(one_hot(wide == lanes_of((LANES, width), start)))
    return jnp.concatenate(tiles, axis=0)


def refined(total, count, weight):
    mean_rows = total * (1.0 / jnp.maximum(count, 1.0))
    lifted = dot(mean_rows.astype(bf16), weight)
    return mean_rows + half_silu(lifted * 0.5)


def widened(column, features):
    return jnp.concatenate([column] * (features // LANES), axis=1)


def put_counts(out_ref, rows, columns):
    features = out_ref.shape[1]
    parts = [col.T[0:1, :] for col in columns]
    parts += [jnp.zeros((1, LANES), f32)] * (features // LANES - len(parts))
    line = jnp.concatenate(parts, axis=1)
    tail = jnp.where(rows_of((PAD, features)) == 0, line, 0.0)
    out_ref[pl.ds(rows, PAD), :] = tail.astype(bf16)


def get_count(tail, c):
    return spread(tail[0:1, c : c + LANES])


def owner_kernel(
    groups,
    cap,
    owners_ref,
    node_rows_hbm,
    near_hbm,
    pair_hbm,
    quad_hbm,
    top_hbm,
    edge_in_hbm,
    edge_bias_hbm,
    node_in_hbm,
    node_bias_hbm,
    arrived,
    dst,
    src,
    raised,
    near_ref,
    two_ref,
    three_ref,
    nodes_ref,
    near_rows,
    pair_ref,
    quads_ref,
    tops_ref,
    edge_in_ref,
    edge_bias_ref,
    node_in_ref,
    node_bias_ref,
    parts,
    sums,
    placed,
    load_sems,
    place_sems,
):
    count, features = arrived.shape
    nodes = nodes_ref.shape[0]
    tile = 256
    a, g = lax.axis_index("sub"), lax.axis_index("grp")
    me = a * groups + g
    owners = count // cap
    per_tile = tile // cap
    tiles = count // tile

    def mesh_place(owner):
        return {"sub": owner // groups, "grp": owner % groups}

    barrier = pltpu.get_barrier_semaphore()

    @pl.loop(0, owners)
    def _(owner):
        @pl.when(owner != me)
        def _():
            pl.semaphore_signal(
                barrier,
                inc=1,
                device_id=mesh_place(owner),
                device_id_type=pl.DeviceIdType.MESH,
            )

    loads = []
    for source, target in (
        (node_rows_hbm, nodes_ref),
        (edge_in_hbm, edge_in_ref),
        (edge_bias_hbm, edge_bias_ref),
        (node_in_hbm.at[0], node_in_ref),
        (node_bias_hbm, node_bias_ref),
        (pair_hbm, pair_ref),
        (quad_hbm, quads_ref),
        (top_hbm, tops_ref),
        (near_hbm.at[0, 0], near_rows),
    ):
        copy = pltpu.make_async_copy(source, target, load_sems.at[len(loads)])
        copy.start()
        loads.append(copy)

    owner_row = owners_ref[...]
    position = jnp.zeros((1, nodes), f32)
    for c in range(0, nodes, LANES):
        column = spread(owners_ref[:, c : c + LANES])
        wide = jnp.concatenate([column] * (nodes // LANES), axis=1)
        shape = (LANES, nodes)
        earlier = (wide == owner_row) & (rows_of(shape, c) < lanes_of(shape))
        position += jnp.sum(jnp.where(earlier, 1.0, 0.0), axis=0, keepdims=True)
    slot_of = owner_row * cap + position.astype(jnp.int32)
    loads[0].wait()
    pl.semaphore_wait(barrier, owners - 1)

    def of_owner(owner):
        return pl.ds(pl.multiple_of(owner * cap, PAD), cap)

    def delivery(owner, sender):
        return pltpu.make_async_remote_copy(
            src_ref=placed.at[of_owner(owner), :],
            dst_ref=arrived.at[of_owner(sender), :],
            send_sem=place_sems.at[0, owner],
            recv_sem=place_sems.at[1, sender],
            device_id=mesh_place(owner),
            device_id_type=pl.DeviceIdType.MESH,
        )

    @pl.loop(0, tiles)
    def _(step):
        t = lax.rem(a + step, tiles)
        start = pl.multiple_of(t * tile, tile)
        weight = jnp.where(rows_of((tile, nodes), start) == slot_of, 1.0, 0.0)
        filled = jnp.max(weight, axis=1, keepdims=True)
        rows = dot(weight.astype(bf16), nodes_ref[...])
        placed[pl.ds(start, tile), :] = jnp.where(filled > 0.5, rows, EMPTY).astype(bf16)

        @pl.loop(0, per_tile)
        def _(k):
            owner = t * per_tile + k

            @pl.when(owner != me)
            def _():
                delivery(owner, me).start()

    arrived[of_owner(me), :] = placed[of_owner(me), :]

    for copy in loads[5:8]:
        copy.wait()
    quad_ref, top_ref = quads_ref.at[a // 2], tops_ref.at[a // 4]

    def compose(outer, inner_row, target_ref):
        which = rows_of((8, count))
        high = (outer >> 7).astype(f32)
        low = (outer & 127).astype(f32)
        parts[...] = jnp.where(which == 0, high, jnp.where(which == 1, low, 0.0))
        sums[...] = jnp.zeros_like(sums)

        @pl.loop(0, tiles)
        def _(t):
            start = pl.multiple_of(t * tile, tile)
            sel = one_hot(rows_of((tile, count), start) == inner_row)
            sums[...] += dot(parts[:, pl.ds(start, tile)].astype(bf16), sel)

        total = sums[...]
        target_ref[...] = (total[0:1] * 128.0 + total[1:2]).astype(jnp.int32)

    compose(pair_ref[...], quad_ref[...], two_ref)
    compose(two_ref[...], top_ref[...], three_ref)
    for copy in loads[1:5] + loads[8:]:
        copy.wait()
    near_count = near_ref.shape[1]

    @pl.loop(0, count // LANES)
    def _(t):
        here = pl.ds(pl.multiple_of(t * LANES, LANES), LANES)
        turned = jnp.concatenate([near_rows[:, here]] * (LANES // near_count), axis=0).T
        near_ref[here, :] = turned[:, 0:near_count]

    @pl.loop(0, tiles)
    def _(step):
        t = lax.rem(a - step + tiles * owners, tiles)

        @pl.loop(0, per_tile)
        def _(k):
            sender = t * per_tile + k

            @pl.when(sender != me)
            def _():
                delivery(me, sender).wait_recv()

        here = pl.ds(pl.multiple_of(t * tile, tile), tile)
        raw = arrived[here, :].astype(f32)
        present = raw[:, 0:1] < LIMIT
        rows = jnp.where(present, raw, 0.0).astype(bf16)
        to_dst = (dot(rows, edge_in_ref[0]) + edge_bias_ref[...]) * 0.5
        dst[here, :] = to_dst.astype(bf16)
        from_src = dot(rows, edge_in_ref[1]) * 0.5
        src[here, :] = jnp.where(present, from_src, AWAY).astype(bf16)
        raised[here, :] = dot(rows, node_in_ref[...]) + node_bias_ref[...]

    @pl.loop(0, owners)
    def _(owner):
        @pl.when(owner != me)
        def _():
            delivery(owner, me).wait_send()


def fine_kernel(
    tile_src_ref,
    arrived,
    dst,
    src,
    raised,
    near_ref,
    edge_out_hbm,
    node_in_hbm,
    node_out_hbm,
    gain_ref,
    fine_ref,
    edge_out_ref,
    node_in_ref,
    node_out_ref,
    agg,
    sels,
    weights,
    near_a,
    near_b,
    load_sems,
):
    count, features = fine_ref.shape
    tile = 256
    tiles = count // tile
    loads = []
    for source, target in (
        (edge_out_hbm, edge_out_ref),
        (node_in_hbm.at[1], node_in_ref),
        (node_out_hbm, node_out_ref),
    ):
        copy = pltpu.make_async_copy(source, target, load_sems.at[len(loads)])
        copy.start()
        loads.append(copy)

    many_near = 4
    pieces_near = TPB * NBR // many_near
    group = 16
    eye = one_hot(rows_of((BLK, BLK)) == lanes_of((BLK, BLK)))
    for p in range(2):
        for i in range(TPB * NBR):
            sels[p, i * BLK : (i + 1) * BLK, BLK : 2 * BLK] = eye

    def gather(b, p, near, i):
        start = pl.multiple_of(b * BLK, BLK)
        j = i * many_near // NBR
        if i * many_near % NBR == 0:
            first = pl.multiple_of(tile_src_ref[0, 0, j, b] * BLK, BLK)
            weights[p, j, 0:BLK, :] = src[pl.ds(first, BLK), :]
            weights[p, j, BLK : 2 * BLK, :] = dst[pl.ds(start, BLK), :]
        which = near_ref[pl.ds(start, BLK), :]
        for k in range(i * many_near, (i + 1) * many_near):
            mask = which[:, k : k + 1] == lanes_of((BLK, BLK))
            sels[p, k * BLK : (k + 1) * BLK, 0:BLK] = one_hot(mask)
        rows = slice(i * many_near * BLK, (i + 1) * many_near * BLK)
        near[rows, :] = dot(sels[p, rows, :], weights[p, j]).astype(bf16)

    def settle(b, near, r):
        total = jnp.zeros((group, features), f32)
        for k in range(0, TPB * NBR, 4):
            terms = [
                half_silu(near[at * BLK + r : at * BLK + r + group, :]) for at in range(k, k + 4)
            ]
            total += ((terms[0] + terms[1]) + (terms[2] + terms[3])).astype(f32)
        agg[pl.ds(pl.multiple_of(b * BLK, BLK) + r, group), :] = total.astype(bf16)

    def both(ahead, p, near_next, b, near):
        for i in range(BLK // group):
            if i % 2 == 0:
                gather(ahead, p, near_next, i * pieces_near // (BLK // group))
            settle(b, near, i * group)

    for i in range(pieces_near):
        gather(0, 0, near_a, i)
    blocks = count // BLK

    @pl.loop(0, blocks // 2)
    def _(h):
        b = 2 * h
        both(b + 1, 1, near_b, b, near_a)
        both(lax.rem(b + 2, blocks), 0, near_a, b + 1, near_b)

    for copy in loads:
        copy.wait()

    @pl.loop(0, tiles)
    def _(t):
        here = pl.ds(pl.multiple_of(t * tile, tile), tile)
        message = dot(agg[here, :], edge_out_ref[...]).astype(bf16)
        lifted = raised[here, :] + dot(message, node_in_ref[...])
        hidden = half_silu(lifted * 0.5).astype(bf16)
        delta = dot(hidden, node_out_ref[...])
        scale = lax.rsqrt(jnp.mean(delta * delta, axis=-1, keepdims=True) + epsilon)
        raw = arrived[here, :].astype(f32)
        fine = raw + gain_ref[...] * (delta * scale)
        fine_ref[here, :] = jnp.where(raw[:, 0:1] < LIMIT, fine, EMPTY).astype(bf16)


def tree_kernel(
    groups,
    fine_ref,
    pair_ref,
    quads_ref,
    tops_ref,
    two_ref,
    three_ref,
    coarse_ref,
    out_ref,
    side,
    partner,
    level_one,
    wide_one,
    mine,
    theirs,
    wide_two,
    packets,
    inbox,
    level_three,
    raised,
    side_sems,
    quad_sems,
    two_sems,
    group_sems,
    spread_sems,
):
    count, features = fine_ref.shape
    half, quarter = count // 2, count // 4
    piece = quarter // groups
    packet = piece + PAD
    tile = 256
    a, g = lax.axis_index("sub"), lax.axis_index("grp")
    quad_ref, top_ref = quads_ref.at[a // 2], tops_ref.at[a // 4]
    core = a + 1 - 2 * (a % 2)
    across = a + 2 - 4 * ((a // 2) % 2)
    others = [lax.rem(g + d, groups) for d in range(1, groups)]
    peers = [{"grp": t} for t in others] + [{"sub": across}, {"sub": core}]
    barrier = pltpu.get_barrier_semaphore()
    for peer in peers:
        pl.semaphore_signal(barrier, inc=1, device_id=peer, device_id_type=pl.DeviceIdType.MESH)

    def send(sems, at, source, target, peer):
        copy = pltpu.make_async_remote_copy(
            src_ref=source,
            dst_ref=target,
            send_sem=sems.at[(0, *at)],
            recv_sem=sems.at[(1, *at)],
            device_id=peer,
            device_id_type=pl.DeviceIdType.MESH,
        )
        copy.start()
        return copy

    many = 512
    sides = []
    for t in range(count // many):
        here = pl.ds(t * many, many)
        sel = picker(pair_ref, t * many, many, 0, count)
        side[here, :] = dot(sel, fine_ref[...]).astype(bf16)
        if t == 0:
            pl.semaphore_wait(barrier, len(peers))
        sides.append(send(side_sems, (t,), side.at[here, :], partner.at[here, :], {"sub": core}))
    for t in range(count // many):
        sides[t].wait_recv()
        for start in range(t * many, (t + 1) * many, tile):
            here = pl.ds(start, tile)
            x = side[here, :].astype(f32)
            y = partner[here, :].astype(f32)
            in_x = x[:, 0:1] < LIMIT
            in_y = y[:, 0:1] < LIMIT
            total = jnp.where(in_x, x, 0.0) + jnp.where(in_y, y, 0.0)
            marks = jnp.where(in_x, 1.0, 0.0) + jnp.where(in_y, 1.0, 0.0)
            level = refined(total, marks, coarse_ref[0]).astype(bf16)
            level_one[here, :] = level
            wide_one[here, 0:features] = level
            wide_one[here, features : features + LANES] = jnp.broadcast_to(
                marks, (tile, LANES)
            ).astype(bf16)

    block = tile + PAD
    quads = []
    for t in range(half // tile):
        sel = picker(quad_ref, (a % 2) * half + t * tile, tile, 0, count)
        got = dot(sel, wide_one[...])
        mine[t * block : t * block + tile, :] = got[:, 0:features].astype(bf16)
        columns = [got[c : c + LANES, features : features + LANES] for c in range(0, tile, LANES)]
        put_counts(mine, t * block + tile, columns)
        here = pl.ds(t * block, block)
        quads.append(send(quad_sems, (t,), mine.at[here, :], theirs.at[here, :], {"sub": across}))

    @pl.loop(0, count // tile)
    def _(t):
        start = pl.multiple_of(t * tile, tile)
        here = pl.ds(start, tile)
        sel = one_hot(rows_of((tile, count), start) == pair_ref[...])
        raised[here, :] = fine_ref[here, :].astype(f32) + dot(sel, level_one[...])

    base = pl.multiple_of((a % 2) * half, half)
    twos = []
    for t in range(half // tile):
        quads[t].wait_recv()
        my_tail = mine[t * block + tile : (t + 1) * block, :].astype(f32)
        their_tail = theirs[t * block + tile : (t + 1) * block, :].astype(f32)
        for c in range(0, tile, LANES):
            x, y = get_count(my_tail, c), get_count(their_tail, c)
            at = t * block + c
            total = widened(x, features) * mine[at : at + LANES, :].astype(f32) + widened(
                y, features
            ) * theirs[at : at + LANES, :].astype(f32)
            level = refined(total, widened(x + y, features), coarse_ref[1])
            there = pl.ds(base + t * tile + c, LANES)
            wide_two[there, 0:features] = level.astype(bf16)
            wide_two[there, features : features + LANES] = (x + y).astype(bf16)
        there = wide_two.at[pl.ds(base + t * tile, tile), :]
        twos.append(send(two_sems, (t,), there, there, {"sub": core}))
    for copy in twos:
        copy.wait_recv()

    sel = picker(top_ref, (a % 4) * quarter, quarter, 0, count)
    got = dot(sel, wide_two[...])
    for t in range(groups):
        at, first = t * packet, t * piece
        packets[at : at + piece, :] = got[first : first + piece, 0:features].astype(bf16)
        columns = [
            got[first + c : first + c + LANES, features : features + LANES]
            for c in range(0, piece, LANES)
        ]
        put_counts(packets, at + piece, columns)
    parcels = []
    for d, t in enumerate(others):
        here = pl.ds(pl.multiple_of(t * packet, PAD), packet)
        parcels.append(
            send(group_sems, (d,), packets.at[here, :], inbox.at[d], {"grp": t})
        )

    @pl.loop(0, count // tile)
    def _(t):
        start = pl.multiple_of(t * tile, tile)
        here = pl.ds(start, tile)
        sel = one_hot(rows_of((tile, count), start) == two_ref[...])
        raised[here, :] += dot(sel, wide_two[:, 0:features])

    for copy in parcels:
        copy.wait_recv()
    own = pl.multiple_of(g * packet, PAD)
    terms = [lambda at, size: packets[pl.ds(own + at, size), :].astype(f32)]
    for d in range(groups - 1):
        terms.append(lambda at, size, d=d: inbox[d, at : at + size, :].astype(f32))
    tails = [term(piece, PAD) for term in terms]
    base_three = pl.multiple_of(((a % 4) * groups + g) * piece, piece)
    for c in range(0, piece, LANES):
        total, marks = 0.0, 0.0
        for term, tail in zip(terms, tails):
            got = get_count(tail, c)
            marks = marks + got
            total = total + widened(got, features) * term(c, LANES)
        level = refined(total, widened(marks, features), coarse_ref[2])
        level_three[pl.ds(base_three + c, LANES), :] = level.astype(bf16)

    def piece_of(sub, group):
        return pl.ds(pl.multiple_of(((sub % 4) * groups + group) * piece, piece), piece)

    def relay(stage, d, rows, peer):
        there = level_three.at[rows, :]
        return send(spread_sems, (stage, d), there, there, peer)

    def lift(sub, last):
        first = pl.multiple_of((sub % 4) * quarter, quarter)

        @pl.loop(0, count // tile)
        def _(t):
            start = pl.multiple_of(t * tile, tile)
            here = pl.ds(start, tile)
            sel = one_hot(rows_of((tile, quarter), start) == three_ref[:, pl.ds(first, quarter)])
            total = raised[here, :] + dot(sel, level_three[pl.ds(first, quarter), :])
            if last:
                present = fine_ref[here, 0:LANES].astype(f32)[:, 0:1] < LIMIT
                out_ref[here, :] = jnp.where(present, total, 0.0).astype(bf16)
            else:
                raised[here, :] = total

    mine_at = piece_of(a, g)
    pieces = [mine_at] + [piece_of(a, lax.rem(g + groups - d, groups)) for d in range(1, groups)]
    thence = [piece_of(across, lax.rem(g + groups - d, groups)) for d in range(groups)]
    over_x = [relay(1, 0, mine_at, {"sub": across})]
    over_z = [relay(0, d, mine_at, {"grp": t}) for d, t in enumerate(others)]
    over_core = [relay(2, 0, mine_at, {"sub": core})]
    for d in range(1, groups):
        over_z[d - 1].wait_recv()
        over_x.append(relay(1, d, pieces[d], {"sub": across}))
        over_core.append(relay(2, d, pieces[d], {"sub": core}))
    lift(a, False)
    relayed = []
    for d in range(groups):
        over_x[d].wait_recv()
        relayed.append(relay(3, d, thence[d], {"sub": core}))
    for copy in over_core:
        copy.wait_recv()
    lift(core, False)
    lift(across, False)
    for copy in relayed:
        copy.wait_recv()
    lift(across + 1 - 2 * (across % 2), True)
    for copy in sides + quads + twos + parcels + over_z + over_x + over_core + relayed:
        copy.wait_send()


def body(
    node_rows,
    owners,
    tile_src,
    neighbors,
    pool_pair,
    pool_quad,
    pool_top,
    edge_in,
    edge_bias,
    edge_out,
    node_in,
    node_bias,
    node_out,
    out_gain,
    coarse,
):
    groups = lax.axis_size("grp")
    owner_count = lax.axis_size("sub") * groups
    count, near_count = neighbors.shape[2:]
    nodes, features = node_rows.shape
    cap = count // owner_count
    half, quarter = count // 2, count // 4
    packet = quarter // groups + PAD
    tile = 256

    def shape(rows, dtype=bf16, width=features):
        return jax.ShapeDtypeStruct((rows, width), dtype)

    def room(like):
        return pltpu.VMEM(like.shape, like.dtype)

    pair = pool_pair.reshape(1, count)
    edge_row, node_row = edge_bias.reshape(1, features), node_bias.reshape(1, features)
    rows = pltpu.VMEM((count, features), bf16)
    sums = pltpu.VMEM((8, count), f32)
    square = pltpu.VMEM((features, features), bf16)
    arrived, dst, src, lifted, near, to_two, to_three = pl.pallas_call(
        functools.partial(owner_kernel, groups, cap),
        out_shape=(
            shape(count),
            shape(count),
            shape(count),
            shape(count, f32),
            jax.ShapeDtypeStruct(neighbors.shape[2:], jnp.int32),
            shape(1, jnp.int32, count),
            shape(1, jnp.int32, count),
        ),
        in_specs=[VM] + [HB] * 9,
        out_specs=(VM,) * 7,
        scratch_shapes=[
            room(node_rows),
            pltpu.VMEM((near_count, count), jnp.int32),
            room(pair),
            room(pool_quad),
            room(pool_top),
            room(edge_in),
            room(edge_row),
            square,
            room(node_row),
            sums,
            sums,
            rows,
            pltpu.SemaphoreType.DMA((9,)),
            pltpu.SemaphoreType.DMA((2, owner_count)),
        ],
        compiler_params=pltpu.CompilerParams(
            collective_id=1, has_side_effects=True, vmem_limit_bytes=24 << 20
        ),
    )(
        owners.reshape(1, nodes),
        node_rows,
        jnp.swapaxes(neighbors, 2, 3),
        pair,
        pool_quad,
        pool_top,
        edge_in,
        edge_row,
        node_in,
        node_row,
    )
    gathered = pltpu.VMEM((TPB * NBR * BLK, features), bf16)
    fine = pl.pallas_call(
        fine_kernel,
        out_shape=shape(count),
        in_specs=[SM] + [VM] * 5 + [HB] * 3 + [VM],
        out_specs=VM,
        scratch_shapes=[square] * 3
        + [
            rows,
            pltpu.VMEM((2, TPB * NBR * BLK, 2 * BLK), bf16),
            pltpu.VMEM((2, TPB, 2 * BLK, features), bf16),
            gathered,
            gathered,
            pltpu.SemaphoreType.DMA((3,)),
        ],
        compiler_params=pltpu.CompilerParams(vmem_limit_bytes=28 << 20),
        cost_estimate=pl.CostEstimate(
            flops=20 * 10**9, bytes_accessed=8 << 20, transcendentals=0
        ),
    )(
        jnp.swapaxes(tile_src, 2, 3),
        arrived,
        dst,
        src,
        lifted,
        near,
        edge_out,
        node_in,
        node_out,
        out_gain.reshape(1, features),
    )
    wide = pltpu.VMEM((count, features + LANES), bf16)
    pooled = pltpu.VMEM((half // tile * (tile + PAD), features), bf16)
    return pl.pallas_call(
        functools.partial(tree_kernel, groups),
        out_shape=shape(count),
        in_specs=[VM] * 7,
        out_specs=VM,
        scratch_shapes=[
            rows,
            rows,
            rows,
            wide,
            pooled,
            pooled,
            wide,
            pltpu.VMEM((groups * packet, features), bf16),
            pltpu.VMEM((groups - 1, packet, features), bf16),
            rows,
            pltpu.VMEM((count, features), f32),
            pltpu.SemaphoreType.DMA((2, count // 512)),
            pltpu.SemaphoreType.DMA((2, half // tile)),
            pltpu.SemaphoreType.DMA((2, half // tile)),
            pltpu.SemaphoreType.DMA((2, groups)),
            pltpu.SemaphoreType.DMA((2, 4, groups)),
        ],
        compiler_params=pltpu.CompilerParams(
            collective_id=0, has_side_effects=True, vmem_limit_bytes=44 << 20
        ),
    )(fine, pair, pool_quad, pool_top, to_two, to_three, coarse)


def solution(mesh):
    in_specs = (
        P(("sub", "grp"), None),
        P(("sub", "grp")),
        P("sub", "grp", None, None),
        P("sub", "grp", None, None),
        P("sub", "grp", None),
        P(None, "grp", None),
        P(None, "grp", None),
        P(),
        P(),
        P(),
        P(),
        P(),
        P(),
        P(),
        P(),
    )
    out_specs = P(("sub", "grp"), None)
    return jax.shard_map(body, mesh=mesh, in_specs=in_specs, out_specs=out_specs, check_vma=False)
```

```python
import functools

import jax
import jax.numpy as jnp
from jax import lax
from jax.experimental import pallas as pl
from jax.experimental.pallas import tpu as pltpu
from jax.sharding import PartitionSpec as P

BLK = 128
TPB = 2
NBR = 8
LANES = 128
PAD = 16
EMPTY = 16384.0
LIMIT = 8192.0
AWAY = -8192.0
epsilon = 1e-05
f32 = jnp.float32
bf16 = jnp.bfloat16

VM = pl.BlockSpec(memory_space=pltpu.VMEM)
SM = pl.BlockSpec(memory_space=pltpu.SMEM)
HB = pl.BlockSpec(memory_space=pltpu.HBM)


def rows_of(shape, start=0):
    return lax.broadcasted_iota(jnp.int32, shape, 0) + start


def lanes_of(shape, start=0):
    return lax.broadcasted_iota(jnp.int32, shape, 1) + start


def one_hot(mask):
    return jnp.where(mask, 1.0, 0.0).astype(bf16)


def spread(row):
    return jnp.broadcast_to(row, (LANES, LANES)).T


def dot(a, b):
    return jnp.dot(a, b, preferred_element_type=f32)


def half_silu(h):
    return h + h * jnp.tanh(h)


def picker(perm_ref, first, count, start, width):
    tiles = []
    for c in range(0, count, LANES):
        column = spread(perm_ref[:, pl.ds(pl.multiple_of(first + c, LANES), LANES)])
        wide = jnp.concatenate([column] * (width // LANES), axis=1)
        tiles.append(one_hot(wide == lanes_of((LANES, width), start)))
    return jnp.concatenate(tiles, axis=0)


def refined(total, count, weight):
    mean_rows = total * (1.0 / jnp.maximum(count, 1.0))
    lifted = dot(mean_rows.astype(bf16), weight)
    return mean_rows + half_silu(lifted * 0.5)


def widened(column, features):
    return jnp.concatenate([column] * (features // LANES), axis=1)


def put_counts(out_ref, rows, columns):
    features = out_ref.shape[1]
    parts = [col.T[0:1, :] for col in columns]
    parts += [jnp.zeros((1, LANES), f32)] * (features // LANES - len(parts))
    line = jnp.concatenate(parts, axis=1)
    tail = jnp.where(rows_of((PAD, features)) == 0, line, 0.0)
    out_ref[pl.ds(rows, PAD), :] = tail.astype(bf16)


def get_count(tail, c):
    return spread(tail[0:1, c : c + LANES])


def slot_kernel(cap, owners_ref, slots_ref):
    nodes = owners_ref.shape[1]
    owner_row = owners_ref[...]
    position = jnp.zeros((1, nodes), f32)
    for c in range(0, nodes, LANES):
        column = spread(owners_ref[:, c : c + LANES])
        wide = jnp.concatenate([column] * (nodes // LANES), axis=1)
        shape = (LANES, nodes)
        earlier = (wide == owner_row) & (rows_of(shape, c) < lanes_of(shape))
        position += jnp.sum(jnp.where(earlier, 1.0, 0.0), axis=0, keepdims=True)
    slots_ref[...] = owner_row * cap + position.astype(jnp.int32)


def owner_kernel(
    groups,
    cap,
    slots_ref,
    node_rows_hbm,
    near_hbm,
    pair_hbm,
    quad_hbm,
    top_hbm,
    edge_in_hbm,
    edge_bias_hbm,
    node_in_hbm,
    node_bias_hbm,
    arrived,
    dst,
    src,
    raised,
    near_ref,
    two_ref,
    three_ref,
    pair_hot,
    nodes_ref,
    near_rows,
    pair_ref,
    quads_ref,
    tops_ref,
    edge_in_ref,
    edge_bias_ref,
    node_in_ref,
    node_bias_ref,
    parts,
    sums,
    placed,
    load_sems,
    place_sems,
):
    count, features = arrived.shape
    nodes = nodes_ref.shape[0]
    tile = 256
    a, g = lax.axis_index("sub"), lax.axis_index("grp")
    me = a * groups + g
    owners = count // cap
    per_tile = tile // cap
    tiles = count // tile

    def mesh_place(owner):
        return {"sub": owner // groups, "grp": owner % groups}

    barrier = pltpu.get_barrier_semaphore()

    @pl.loop(0, owners)
    def _(owner):
        @pl.when(owner != me)
        def _():
            pl.semaphore_signal(
                barrier,
                inc=1,
                device_id=mesh_place(owner),
                device_id_type=pl.DeviceIdType.MESH,
            )

    loads = []
    for source, target in (
        (node_rows_hbm, nodes_ref),
        (edge_in_hbm, edge_in_ref),
        (edge_bias_hbm, edge_bias_ref),
        (node_in_hbm.at[0], node_in_ref),
        (node_bias_hbm, node_bias_ref),
        (pair_hbm, pair_ref),
        (quad_hbm, quads_ref),
        (top_hbm, tops_ref),
        (near_hbm.at[0, 0], near_rows),
    ):
        copy = pltpu.make_async_copy(source, target, load_sems.at[len(loads)])
        copy.start()
        loads.append(copy)

    slot_of = slots_ref[...]
    loads[0].wait()
    pl.semaphore_wait(barrier, owners - 1)

    def of_owner(owner):
        return pl.ds(pl.multiple_of(owner * cap, PAD), cap)

    def delivery(owner, sender):
        return pltpu.make_async_remote_copy(
            src_ref=placed.at[of_owner(owner), :],
            dst_ref=arrived.at[of_owner(sender), :],
            send_sem=place_sems.at[0, owner],
            recv_sem=place_sems.at[1, sender],
            device_id=mesh_place(owner),
            device_id_type=pl.DeviceIdType.MESH,
        )

    @pl.loop(0, tiles)
    def _(step):
        t = lax.rem(a + step, tiles)
        start = pl.multiple_of(t * tile, tile)
        weight = jnp.where(rows_of((tile, nodes), start) == slot_of, 1.0, 0.0)
        filled = jnp.max(weight, axis=1, keepdims=True)
        rows = dot(weight.astype(bf16), nodes_ref[...])
        placed[pl.ds(start, tile), :] = jnp.where(filled > 0.5, rows, EMPTY).astype(bf16)

        @pl.loop(0, per_tile)
        def _(k):
            owner = t * per_tile + k

            @pl.when(owner != me)
            def _():
                delivery(owner, me).start()

    arrived[of_owner(me), :] = placed[of_owner(me), :]

    for copy in loads[5:8]:
        copy.wait()
    quad_ref, top_ref = quads_ref.at[a // 2], tops_ref.at[a // 4]

    def compose(outer, inner_row, target_ref):
        which = rows_of((8, count))
        high = (outer >> 7).astype(f32)
        low = (outer & 127).astype(f32)
        parts[...] = jnp.where(which == 0, high, jnp.where(which == 1, low, 0.0))
        sums[...] = jnp.zeros_like(sums)

        @pl.loop(0, tiles)
        def _(t):
            start = pl.multiple_of(t * tile, tile)
            sel = one_hot(rows_of((tile, count), start) == inner_row)
            sums[...] += dot(parts[:, pl.ds(start, tile)].astype(bf16), sel)

        total = sums[...]
        target_ref[...] = (total[0:1] * 128.0 + total[1:2]).astype(jnp.int32)

    compose(pair_ref[...], quad_ref[...], two_ref)
    compose(two_ref[...], top_ref[...], three_ref)
    for copy in loads[1:5] + loads[8:]:
        copy.wait()
    near_count = near_ref.shape[1]

    @pl.loop(0, tiles)
    def _(t):
        start = pl.multiple_of(t * tile, tile)
        pair_hot[pl.ds(start, tile), :] = picker(pair_ref, start, tile, 0, count)

    @pl.loop(0, count // LANES)
    def _(t):
        here = pl.ds(pl.multiple_of(t * LANES, LANES), LANES)
        turned = jnp.concatenate([near_rows[:, here]] * (LANES // near_count), axis=0).T
        near_ref[here, :] = turned[:, 0:near_count]

    @pl.loop(0, tiles)
    def _(step):
        t = lax.rem(a - step + tiles * owners, tiles)

        @pl.loop(0, per_tile)
        def _(k):
            sender = t * per_tile + k

            @pl.when(sender != me)
            def _():
                delivery(me, sender).wait_recv()

        here = pl.ds(pl.multiple_of(t * tile, tile), tile)
        raw = arrived[here, :].astype(f32)
        present = raw[:, 0:1] < LIMIT
        rows = jnp.where(present, raw, 0.0).astype(bf16)
        to_dst = (dot(rows, edge_in_ref[0]) + edge_bias_ref[...]) * 0.5
        dst[here, :] = to_dst.astype(bf16)
        from_src = dot(rows, edge_in_ref[1]) * 0.5
        src[here, :] = jnp.where(present, from_src, AWAY).astype(bf16)
        raised[here, :] = dot(rows, node_in_ref[...]) + node_bias_ref[...]

    @pl.loop(0, owners)
    def _(owner):
        @pl.when(owner != me)
        def _():
            delivery(owner, me).wait_send()


def refined(total, count, weight):
    mean_rows = total * (1.0 / jnp.maximum(count, 1.0))
    lifted = dot(mean_rows.astype(bf16), weight)
    return mean_rows + half_silu(lifted * 0.5)


def widened(column, features):
    return jnp.concatenate([column] * (features // LANES), axis=1)


def put_counts(out_ref, rows, columns):
    features = out_ref.shape[1]
    parts = [col.T[0:1, :] for col in columns]
    parts += [jnp.zeros((1, LANES), f32)] * (features // LANES - len(parts))
    line = jnp.concatenate(parts, axis=1)
    tail = jnp.where(rows_of((PAD, features)) == 0, line, 0.0)
    out_ref[pl.ds(rows, PAD), :] = tail.astype(bf16)


def get_count(tail, c):
    return spread(tail[0:1, c : c + LANES])


def slot_kernel(cap, owners_ref, slots_ref):
    nodes = owners_ref.shape[1]
    owner_row = owners_ref[...]
    position = jnp.zeros((1, nodes), f32)
    for c in range(0, nodes, LANES):
        column = spread(owners_ref[:, c : c + LANES])
        wide = jnp.concatenate([column] * (nodes // LANES), axis=1)
        shape = (LANES, nodes)
        earlier = (wide == owner_row) & (rows_of(shape, c) < lanes_of(shape))
        position += jnp.sum(jnp.where(earlier, 1.0, 0.0), axis=0, keepdims=True)
    slots_ref[...] = owner_row * cap + position.astype(jnp.int32)


def owner_kernel(
    groups,
    cap,
    slots_ref,
    node_rows_hbm,
    near_hbm,
    pair_hbm,
    quad_hbm,
    top_hbm,
    edge_in_hbm,
    edge_bias_hbm,
    node_in_hbm,
    node_bias_hbm,
    arrived,
    dst,
    src,
    raised,
    near_ref,
    two_ref,
    three_ref,
    pair_hot,
    nodes_ref,
    near_rows,
    pair_ref,
    quads_ref,
    tops_ref,
    edge_in_ref,
    edge_bias_ref,
    node_in_ref,
    node_bias_ref,
    parts,
    sums,
    placed,
    load_sems,
    place_sems,
):
    count, features = arrived.shape
    nodes = nodes_ref.shape[0]
    tile = 256
    a, g = lax.axis_index("sub"), lax.axis_index("grp")
    me = a * groups + g
    owners = count // cap
    per_tile = tile // cap
    tiles = count // tile

    def mesh_place(owner):
        return {"sub": owner // groups, "grp": owner % groups}

    barrier = pltpu.get_barrier_semaphore()

    @pl.loop(0, owners)
    def _(owner):
        @pl.when(owner != me)
        def _():
            pl.semaphore_signal(
                barrier,
                inc=1,
                device_id=mesh_place(owner),
                device_id_type=pl.DeviceIdType.MESH,
            )

    loads = []
    for source, target in (
        (node_rows_hbm, nodes_ref),
        (edge_in_hbm, edge_in_ref),
        (edge_bias_hbm, edge_bias_ref),
        (node_in_hbm.at[0], node_in_ref),
        (node_bias_hbm, node_bias_ref),
        (pair_hbm, pair_ref),
        (quad_hbm, quads_ref),
        (top_hbm, tops_ref),
        (near_hbm.at[0, 0], near_rows),
    ):
        copy = pltpu.make_async_copy(source, target, load_sems.at[len(loads)])
        copy.start()
        loads.append(copy)

    slot_of = slots_ref[...]
    loads[0].wait()
    pl.semaphore_wait(barrier, owners - 1)

    def of_owner(owner):
        return pl.ds(pl.multiple_of(owner * cap, PAD), cap)

    def delivery(owner, sender):
        return pltpu.make_async_remote_copy(
            src_ref=placed.at[of_owner(owner), :],
            dst_ref=arrived.at[of_owner(sender), :],
            send_sem=place_sems.at[0, owner],
            recv_sem=place_sems.at[1, sender],
            device_id=mesh_place(owner),
            device_id_type=pl.DeviceIdType.MESH,
        )

    @pl.loop(0, tiles)
    def _(step):
        t = lax.rem(a + step, tiles)
        start = pl.multiple_of(t * tile, tile)
        weight = jnp.where(rows_of((tile, nodes), start) == slot_of, 1.0, 0.0)
        filled = jnp.max(weight, axis=1, keepdims=True)
        rows = dot(weight.astype(bf16), nodes_ref[...])
        placed[pl.ds(start, tile), :] = jnp.where(filled > 0.5, rows, EMPTY).astype(bf16)

        @pl.loop(0, per_tile)
        def _(k):
            owner = t * per_tile + k

            @pl.when(owner != me)
            def _():
                delivery(owner, me).start()

    arrived[of_owner(me), :] = placed[of_owner(me), :]

    for copy in loads[5:8]:
        copy.wait()
    quad_ref, top_ref = quads_ref.at[a // 2], tops_ref.at[a // 4]

    def compose(outer, inner_row, target_ref):
        which = rows_of((8, count))
        high = (outer >> 7).astype(f32)
        low = (outer & 127).astype(f32)
        parts[...] = jnp.where(which == 0, high, jnp.where(which == 1, low, 0.0))
        sums[...] = jnp.zeros_like(sums)

        @pl.loop(0, tiles)
        def _(t):
            start = pl.multiple_of(t * tile, tile)
            sel = one_hot(rows_of((tile, count), start) == inner_row)
            sums[...] += dot(parts[:, pl.ds(start, tile)].astype(bf16), sel)

        total = sums[...]
        target_ref[...] = (total[0:1] * 128.0 + total[1:2]).astype(jnp.int32)

    compose(pair_ref[...], quad_ref[...], two_ref)
    compose(two_ref[...], top_ref[...], three_ref)
    for copy in loads[1:5] + loads[8:]:
        copy.wait()
    near_count = near_ref.shape[1]

    @pl.loop(0, tiles)
    def _(t):
        start = pl.multiple_of(t * tile, tile)
        pair_hot[pl.ds(start, tile), :] = picker(pair_ref, start, tile, 0, count)

    @pl.loop(0, count // LANES)
    def _(t):
        here = pl.ds(pl.multiple_of(t * LANES, LANES), LANES)
        turned = jnp.concatenate([near_rows[:, here]] * (LANES // near_count), axis=0).T
        near_ref[here, :] = turned[:, 0:near_count]

    @pl.loop(0, tiles)
    def _(step):
        t = lax.rem(a - step + tiles * owners, tiles)

        @pl.loop(0, per_tile)
        def _(k):
            sender = t * per_tile + k

            @pl.when(sender != me)
            def _():
                delivery(me, sender).wait_recv()

        here = pl.ds(pl.multiple_of(t * tile, tile), tile)
        raw = arrived[here, :].astype(f32)
        present = raw[:, 0:1] < LIMIT
        rows = jnp.where(present, raw, 0.0).astype(bf16)
        to_dst = (dot(rows, edge_in_ref[0]) + edge_bias_ref[...]) * 0.5
        dst[here, :] = to_dst.astype(bf16)
        from_src = dot(rows, edge_in_ref[1]) * 0.5
        src[here, :] = jnp.where(present, from_src, AWAY).astype(bf16)
        raised[here, :] = dot(rows, node_in_ref[...]) + node_bias_ref[...]

    @pl.loop(0, owners)
    def _(owner):
        @pl.when(owner != me)
        def _():
            delivery(owner, me).wait_send()


def fine_kernel(
    tile_src_ref,
    arrived,
    dst,
    src,
    raised,
    near_ref,
    edge_out_hbm,
    node_in_hbm,
    node_out_hbm,
    gain_ref,
    fine_ref,
    edge_out_ref,
    node_in_ref,
    node_out_ref,
    agg,
    sels,
    weights,
    near_a,
    near_b,
    load_sems,
):
    count, features = fine_ref.shape
    tile = 256
    tiles = count // tile
    loads = []
    for source, target in (
        (edge_out_hbm, edge_out_ref),
        (node_in_hbm.at[1], node_in_ref),
        (node_out_hbm, node_out_ref),
    ):
        copy = pltpu.make_async_copy(source, target, load_sems.at[len(loads)])
        copy.start()
        loads.append(copy)

    many_near = 4
    pieces_near = TPB * NBR // many_near
    group = 16
    eye = one_hot(rows_of((BLK, BLK)) == lanes_of((BLK, BLK)))
    for p in range(2):
        for i in range(TPB * NBR):
            sels[p, i * BLK : (i + 1) * BLK, BLK : 2 * BLK] = eye

    def gather(b, p, near, i):
        start = pl.multiple_of(b * BLK, BLK)
        j = i * many_near // NBR
        if i * many_near % NBR == 0:
            first = pl.multiple_of(tile_src_ref[0, 0, j, b] * BLK, BLK)
            weights[p, j, 0:BLK, :] = src[pl.ds(first, BLK), :]
            weights[p, j, BLK : 2 * BLK, :] = dst[pl.ds(start, BLK), :]
        which = near_ref[pl.ds(start, BLK), :]
        for k in range(i * many_near, (i + 1) * many_near):
            mask = which[:, k : k + 1] == lanes_of((BLK, BLK))
            sels[p, k * BLK : (k + 1) * BLK, 0:BLK] = one_hot(mask)
        rows = slice(i * many_near * BLK, (i + 1) * many_near * BLK)
        near[rows, :] = dot(sels[p, rows, :], weights[p, j]).astype(bf16)

    def settle(b, near, r):
        total = jnp.zeros((group, features), f32)
        for k in range(0, TPB * NBR, 4):
            terms = [
                half_silu(near[at * BLK + r : at * BLK + r + group, :]) for at in range(k, k + 4)
            ]
            total += ((terms[0] + terms[1]) + (terms[2] + terms[3])).astype(f32)
        agg[pl.ds(pl.multiple_of(b * BLK, BLK) + r, group), :] = total.astype(bf16)

    def both(ahead, p, near_next, b, near):
        for i in range(BLK // group):
            if i % 2 == 0:
                gather(ahead, p, near_next, i * pieces_near // (BLK // group))
            settle(b, near, i * group)

    for i in range(pieces_near):
        gather(0, 0, near_a, i)
    blocks = count // BLK

    @pl.loop(0, blocks // 2)
    def _(h):
        b = 2 * h
        both(b + 1, 1, near_b, b, near_a)
        both(lax.rem(b + 2, blocks), 0, near_a, b + 1, near_b)

    for copy in loads:
        copy.wait()

    many = 512

    @pl.loop(0, count // many)
    def _(t):
        here = pl.ds(pl.multiple_of(t * many, many), many)
        message = dot(agg[here, :], edge_out_ref[...]).astype(bf16)
        lifted = raised[here, :] + dot(message, node_in_ref[...])
        hidden = half_silu(lifted * 0.5).astype(bf16)
        delta = dot(hidden, node_out_ref[...])
        scale = lax.rsqrt(jnp.mean(delta * delta, axis=-1, keepdims=True) + epsilon)
        raw = arrived[here, :].astype(f32)
        fine = raw + gain_ref[...] * (delta * scale)
        fine_ref[here, :] = jnp.where(raw[:, 0:1] < LIMIT, fine, EMPTY).astype(bf16)


def tree_kernel(
    groups,
    fine_ref,
    pair_ref,
    pair_hot,
    quads_ref,
    tops_ref,
    two_ref,
    three_ref,
    coarse_ref,
    out_ref,
    side,
    partner,
    level_one,
    wide_one,
    mine,
    theirs,
    wide_two,
    packets,
    inbox,
    level_three,
    raised,
    top_hot,
    side_sems,
    quad_sems,
    two_sems,
    group_sems,
    spread_sems,
):
    count, features = fine_ref.shape
    half, quarter = count // 2, count // 4
    piece = quarter // groups
    packet = piece + PAD
    tile, big = 256, 512
    a, g = lax.axis_index("sub"), lax.axis_index("grp")
    quad_ref, top_ref = quads_ref.at[a // 2], tops_ref.at[a // 4]
    core = a + 1 - 2 * (a % 2)
    across = a + 2 - 4 * ((a // 2) % 2)
    others = [lax.rem(g + d, groups) for d in range(1, groups)]
    peers = [{"grp": t} for t in others] + [{"sub": across}, {"sub": core}]
    barrier = pltpu.get_barrier_semaphore()
    for peer in peers:
        pl.semaphore_signal(barrier, inc=1, device_id=peer, device_id_type=pl.DeviceIdType.MESH)

    def send(sems, at, source, target, peer):
        copy = pltpu.make_async_remote_copy(
            src_ref=source,
            dst_ref=target,
            send_sem=sems.at[(0, *at)],
            recv_sem=sems.at[(1, *at)],
            device_id=peer,
            device_id_type=pl.DeviceIdType.MESH,
        )
        copy.start()
        return copy

    many = 1024
    sides = []
    for t in range(count // many):
        here = pl.ds(t * many, many)
        side[here, :] = dot(pair_hot[here, :], fine_ref[...]).astype(bf16)
        if t == 0:
            pl.semaphore_wait(barrier, len(peers))
        sides.append(send(side_sems, (t,), side.at[here, :], partner.at[here, :], {"sub": core}))
    for t in range(count // many):
        sides[t].wait_recv()
        for start in range(t * many, (t + 1) * many, big):
            here = pl.ds(start, big)
            x = side[here, :].astype(f32)
            y = partner[here, :].astype(f32)
            in_x = x[:, 0:1] < LIMIT
            in_y = y[:, 0:1] < LIMIT
            total = jnp.where(in_x, x, 0.0) + jnp.where(in_y, y, 0.0)
            marks = jnp.where(in_x, 1.0, 0.0) + jnp.where(in_y, 1.0, 0.0)
            level = refined(total, marks, coarse_ref[0]).astype(bf16)
            level_one[here, :] = level
            wide_one[here, 0:features] = level
            wide_one[here, features : features + LANES] = jnp.broadcast_to(
                marks, (big, LANES)
            ).astype(bf16)

    block = tile + PAD
    quads = []
    for t in range(half // tile):
        sel = picker(quad_ref, (a % 2) * half + t * tile, tile, 0, count)
        got = dot(sel, wide_one[...])
        mine[t * block : t * block + tile, :] = got[:, 0:features].astype(bf16)
        columns = [got[c : c + LANES, features : features + LANES] for c in range(0, tile, LANES)]
        put_counts(mine, t * block + tile, columns)
        here = pl.ds(t * block, block)
        quads.append(send(quad_sems, (t,), mine.at[here, :], theirs.at[here, :], {"sub": across}))

    @pl.loop(0, count // big)
    def _(t):
        start = pl.multiple_of(t * big, big)
        here = pl.ds(start, big)
        sel = one_hot(rows_of((big, count), start) == pair_ref[...])
        raised[here, :] = fine_ref[here, :].astype(f32) + dot(sel, level_one[...])

    top_hot[...] = picker(top_ref, (a % 4) * quarter, quarter, 0, count)
    base = pl.multiple_of((a % 2) * half, half)
    twos = []
    for t in range(half // tile):
        quads[t].wait_recv()
        my_tail = mine[t * block + tile : (t + 1) * block, :].astype(f32)
        their_tail = theirs[t * block + tile : (t + 1) * block, :].astype(f32)
        for c in range(0, tile, LANES):
            x, y = get_count(my_tail, c), get_count(their_tail, c)
            at = t * block + c
            total = widened(x, features) * mine[at : at + LANES, :].astype(f32) + widened(
                y, features
            ) * theirs[at : at + LANES, :].astype(f32)
            level = refined(total, widened(x + y, features), coarse_ref[1])
            there = pl.ds(base + t * tile + c, LANES)
            wide_two[there, 0:features] = level.astype(bf16)
            wide_two[there, features : features + LANES] = (x + y).astype(bf16)
        there = wide_two.at[pl.ds(base + t * tile, tile), :]
        twos.append(send(two_sems, (t,), there, there, {"sub": core}))
    for copy in twos:
        copy.wait_recv()

    got = dot(top_hot[...], wide_two[...])
    for t in range(groups):
        at, first = t * packet, t * piece
        packets[at : at + piece, :] = got[first : first + piece, 0:features].astype(bf16)
        columns = [
            got[first + c : first + c + LANES, features : features + LANES]
            for c in range(0, piece, LANES)
        ]
        put_counts(packets, at + piece, columns)
    parcels = []
    for d, t in enumerate(others):
        here = pl.ds(pl.multiple_of(t * packet, PAD), packet)
        parcels.append(
            send(group_sems, (d,), packets.at[here, :], inbox.at[d], {"grp": t})
        )

    @pl.loop(0, count // big)
    def _(t):
        start = pl.multiple_of(t * big, big)
        here = pl.ds(start, big)
        sel = one_hot(rows_of((big, count), start) == two_ref[...])
        raised[here, :] += dot(sel, wide_two[:, 0:features])

    for copy in parcels:
        copy.wait_recv()
    own = pl.multiple_of(g * packet, PAD)
    terms = [lambda at, size: packets[pl.ds(own + at, size), :].astype(f32)]
    for d in range(groups - 1):
        terms.append(lambda at, size, d=d: inbox[d, at : at + size, :].astype(f32))
    tails = [term(piece, PAD) for term in terms]

    def piece_of(sub, group):
        return pl.ds(pl.multiple_of((group * 4 + sub % 4) * piece, piece), piece)

    base_three = pl.multiple_of((g * 4 + a % 4) * piece, piece)
    for c in range(0, piece, LANES):
        total, marks = 0.0, 0.0
        for term, tail in zip(terms, tails):
            got = get_count(tail, c)
            marks = marks + got
            total = total + widened(got, features) * term(c, LANES)
        level = refined(total, widened(marks, features), coarse_ref[2])
        level_three[pl.ds(base_three + c, LANES), :] = level.astype(bf16)

    near = g + 1 - 2 * (g % 2)
    order = [g, near, 2 - g // 2, 3 - 3 * (g // 2)]

    def relay(stage, leaves, comes, rows, peer):
        there = level_three.at[rows, :]
        return pltpu.make_async_remote_copy(
            src_ref=there,
            dst_ref=there,
            send_sem=spread_sems.at[0, stage, leaves],
            recv_sem=spread_sems.at[1, stage, comes],
            device_id=peer,
            device_id_type=pl.DeviceIdType.MESH,
        )

    def lift(group, sub, subs, last):
        targets = jnp.concatenate(
            [
                three_ref[:, pl.ds(pl.multiple_of((i * groups + group) * piece, piece), piece)]
                for i in [sub + j for j in range(subs)]
            ],
            axis=1,
        )
        width = subs * piece
        rows = pl.ds(pl.multiple_of((group * 4 + sub) * piece, piece), width)

        @pl.loop(0, count // big)
        def _(t):
            start = pl.multiple_of(t * big, big)
            here = pl.ds(start, big)
            sel = one_hot(rows_of((big, width), start) == targets)
            total = raised[here, :] + dot(sel, level_three[rows, :])
            if last:
                present = fine_ref[here, 0:LANES].astype(f32)[:, 0:1] < LIMIT
                out_ref[here, :] = jnp.where(present, total, 0.0).astype(bf16)
            else:
                raised[here, :] = total

    over_x, over_core, relayed = [], [], []

    def pass_on(group):
        over_x.append(relay(1, group, group, piece_of(a, group), {"sub": across}))
        over_x[-1].start()
        over_core.append(relay(2, group, group, piece_of(a, group), {"sub": core}))
        over_core[-1].start()

    def finish(k, last):
        group = order[k]
        over_x[k].wait_recv()
        relayed.append(relay(3, group, group, piece_of(across, group), {"sub": core}))
        relayed[k].start()
        over_core[k].wait_recv()
        if last:
            pair = (a % 4) // 2 * 2
            lift(group, pair, 2, False)
            relayed[k].wait_recv()
            lift(group, 2 - pair, 2, True)
        else:
            relayed[k].wait_recv()
            lift(group, 0, 4, False)

    mine_at = piece_of(a, g)
    pass_on(g)
    over_z = [relay(0, t, g, mine_at, {"grp": t}) for t in order[1:]]
    for copy in over_z:
        copy.start()
    for k in range(1, groups):
        source = order[k]
        relay(0, source, source, piece_of(a, source), {"grp": source}).wait_recv()
        pass_on(source)
        finish(k - 1, False)
    finish(groups - 1, True)
    for copy in sides + quads + twos + parcels + over_z + over_x + over_core + relayed:
        copy.wait_send()


def body(
    node_rows,
    owners,
    tile_src,
    neighbors,
    pool_pair,
    pool_quad,
    pool_top,
    edge_in,
    edge_bias,
    edge_out,
    node_in,
    node_bias,
    node_out,
    out_gain,
    coarse,
):
    groups = lax.axis_size("grp")
    owner_count = lax.axis_size("sub") * groups
    count, near_count = neighbors.shape[2:]
    nodes, features = node_rows.shape
    cap = count // owner_count
    half, quarter = count // 2, count // 4
    packet = quarter // groups + PAD
    tile = 256

    def shape(rows, dtype=bf16, width=features):
        return jax.ShapeDtypeStruct((rows, width), dtype)

    def room(like):
        return pltpu.VMEM(like.shape, like.dtype)

    pair = pool_pair.reshape(1, count)
    edge_row, node_row = edge_bias.reshape(1, features), node_bias.reshape(1, features)
    rows = pltpu.VMEM((count, features), bf16)
    sums = pltpu.VMEM((8, count), f32)
    square = pltpu.VMEM((features, features), bf16)
    slots = pl.pallas_call(
        functools.partial(slot_kernel, cap),
        out_shape=shape(1, jnp.int32, nodes),
        in_specs=[VM],
        out_specs=VM,
        compiler_params=pltpu.CompilerParams(vmem_limit_bytes=8 << 20),
        cost_estimate=pl.CostEstimate(
            flops=20 * 10**9, bytes_accessed=8 << 20, transcendentals=0
        ),
    )(owners.reshape(1, nodes))
    arrived, dst, src, lifted, near, to_two, to_three, pair_hot = pl.pallas_call(
        functools.partial(owner_kernel, groups, cap),
        out_shape=(
            shape(count),
            shape(count),
            shape(count),
            shape(count, f32),
            jax.ShapeDtypeStruct(neighbors.shape[2:], jnp.int32),
            shape(1, jnp.int32, count),
            shape(1, jnp.int32, count),
            shape(count, bf16, count),
        ),
        in_specs=[VM] + [HB] * 9,
        out_specs=(VM,) * 8,
        scratch_shapes=[
            room(node_rows),
            pltpu.VMEM((near_count, count), jnp.int32),
            room(pair),
            room(pool_quad),
            room(pool_top),
            room(edge_in),
            room(edge_row),
            square,
            room(node_row),
            sums,
            sums,
            rows,
            pltpu.SemaphoreType.DMA((9,)),
            pltpu.SemaphoreType.DMA((2, owner_count)),
        ],
        compiler_params=pltpu.CompilerParams(
            collective_id=1, has_side_effects=True, vmem_limit_bytes=24 << 20
        ),
    )(
        slots,
        node_rows,
        jnp.swapaxes(neighbors, 2, 3),
        pair,
        pool_quad,
        pool_top,
        edge_in,
        edge_row,
        node_in,
        node_row,
    )
    gathered = pltpu.VMEM((TPB * NBR * BLK, features), bf16)
    fine = pl.pallas_call(
        fine_kernel,
        out_shape=shape(count),
        in_specs=[SM] + [VM] * 5 + [HB] * 3 + [VM],
        out_specs=VM,
        scratch_shapes=[square] * 3
        + [
            rows,
            pltpu.VMEM((2, TPB * NBR * BLK, 2 * BLK), bf16),
            pltpu.VMEM((2, TPB, 2 * BLK, features), bf16),
            gathered,
            gathered,
            pltpu.SemaphoreType.DMA((3,)),
        ],
        compiler_params=pltpu.CompilerParams(vmem_limit_bytes=28 << 20),
        cost_estimate=pl.CostEstimate(
            flops=20 * 10**9, bytes_accessed=8 << 20, transcendentals=0
        ),
    )(
        jnp.swapaxes(tile_src, 2, 3),
        arrived,
        dst,
        src,
        lifted,
        near,
        edge_out,
        node_in,
        node_out,
        out_gain.reshape(1, features),
    )
    wide = pltpu.VMEM((count, features + LANES), bf16)
    pooled = pltpu.VMEM((half // tile * (tile + PAD), features), bf16)
    return pl.pallas_call(
        functools.partial(tree_kernel, groups),
        out_shape=shape(count),
        in_specs=[VM] * 8,
        out_specs=VM,
        scratch_shapes=[
            rows,
            rows,
            rows,
            wide,
            pooled,
            pooled,
            wide,
            pltpu.VMEM((groups * packet, features), bf16),
            pltpu.VMEM((groups - 1, packet, features), bf16),
            rows,
            pltpu.VMEM((count, features), f32),
            pltpu.VMEM((quarter, count), bf16),
            pltpu.SemaphoreType.DMA((2, count // 1024)),
            pltpu.SemaphoreType.DMA((2, half // tile)),
            pltpu.SemaphoreType.DMA((2, half // tile)),
            pltpu.SemaphoreType.DMA((2, groups)),
            pltpu.SemaphoreType.DMA((2, 4, groups)),
        ],
        compiler_params=pltpu.CompilerParams(
            collective_id=0, has_side_effects=True, vmem_limit_bytes=40 << 20
        ),
    )(fine, pair, pair_hot, pool_quad, pool_top, to_two, to_three, coarse)


def solution(mesh):
    in_specs = (
        P(("sub", "grp"), None),
        P(("sub", "grp")),
        P("sub", "grp", None, None),
        P("sub", "grp", None, None),
        P("sub", "grp", None),
        P(None, "grp", None),
        P(None, "grp", None),
        P(),
        P(),
        P(),
        P(),
        P(),
        P(),
        P(),
        P(),
    )
    out_specs = P(("sub", "grp"), None)
    return jax.shard_map(body, mesh=mesh, in_specs=in_specs, out_specs=out_specs, check_vma=False)
```

```python
import functools

import jax
import jax.numpy as jnp
from jax import lax
from jax.experimental import pallas as pl
from jax.experimental.pallas import tpu as pltpu
from jax.sharding import PartitionSpec as P

BLK = 128
TPB = 2
NBR = 8
LANES = 128
PAD = 16
MARKS = 8
EMPTY = 16384.0
LIMIT = 8192.0
AWAY = -8192.0
epsilon = 1e-05
f32 = jnp.float32
bf16 = jnp.bfloat16

VM = pl.BlockSpec(memory_space=pltpu.VMEM)
SM = pl.BlockSpec(memory_space=pltpu.SMEM)
HB = pl.BlockSpec(memory_space=pltpu.HBM)


def rows_of(shape, start=0):
    return lax.broadcasted_iota(jnp.int32, shape, 0) + start


def lanes_of(shape, start=0):
    return lax.broadcasted_iota(jnp.int32, shape, 1) + start


def one_hot(mask):
    return jnp.where(mask, 1.0, 0.0).astype(bf16)


def spread(row):
    return jnp.broadcast_to(row, (LANES, LANES)).T


def dot(a, b):
    return jnp.dot(a, b, preferred_element_type=f32)


def half_silu(h):
    return h + h * jnp.tanh(h)


def picker(perm_ref, first, count, start, width):
    tiles = []
    for c in range(0, count, LANES):
        column = spread(perm_ref[:, pl.ds(pl.multiple_of(first + c, LANES), LANES)])
        wide = jnp.concatenate([column] * (width // LANES), axis=1)
        tiles.append(one_hot(wide == lanes_of((LANES, width), start)))
    return jnp.concatenate(tiles, axis=0)


def refined(total, count, weight):
    mean_rows = total * (1.0 / jnp.maximum(count, 1.0))
    lifted = dot(mean_rows.astype(bf16), weight)
    return mean_rows + half_silu(lifted * 0.5)


def widened(column, features):
    return jnp.concatenate([column] * (features // LANES), axis=1)


def put_marks(out_ref, at, columns):
    lines = [col.T[0:1, :] for col in columns]
    lines.append(jnp.zeros((MARKS - len(lines), LANES), f32))
    out_ref[at] = jnp.concatenate(lines, axis=0)


def slot_kernel(cap, owners_ref, slots_ref):
    nodes = owners_ref.shape[1]
    owner_row = owners_ref[...]
    position = jnp.zeros((1, nodes), f32)
    for c in range(0, nodes, LANES):
        column = spread(owners_ref[:, c : c + LANES])
        wide = jnp.concatenate([column] * (nodes // LANES), axis=1)
        shape = (LANES, nodes)
        earlier = (wide == owner_row) & (rows_of(shape, c) < lanes_of(shape))
        position += jnp.sum(jnp.where(earlier, 1.0, 0.0), axis=0, keepdims=True)
    slots_ref[...] = owner_row * cap + position.astype(jnp.int32)


def owner_kernel(
    groups,
    cap,
    slots_ref,
    node_rows_hbm,
    near_hbm,
    pair_hbm,
    quad_hbm,
    top_hbm,
    edge_in_hbm,
    edge_bias_hbm,
    node_in_hbm,
    node_bias_hbm,
    arrived,
    dst,
    src,
    raised,
    near_ref,
    two_ref,
    three_ref,
    pair_hot,
    nodes_ref,
    near_rows,
    pair_ref,
    quads_ref,
    tops_ref,
    edge_in_ref,
    edge_bias_ref,
    node_in_ref,
    node_bias_ref,
    parts,
    sums,
    placed,
    load_sems,
    place_sems,
):
    count, features = arrived.shape
    nodes = nodes_ref.shape[0]
    tile = 256
    a, g = lax.axis_index("sub"), lax.axis_index("grp")
    me = a * groups + g
    owners = count // cap
    per_tile = tile // cap
    tiles = count // tile

    def mesh_place(owner):
        return {"sub": owner // groups, "grp": owner % groups}

    barrier = pltpu.get_barrier_semaphore()

    @pl.loop(0, owners)
    def _(owner):
        @pl.when(owner != me)
        def _():
            pl.semaphore_signal(
                barrier,
                inc=1,
                device_id=mesh_place(owner),
                device_id_type=pl.DeviceIdType.MESH,
            )

    loads = []
    for source, target in (
        (node_rows_hbm, nodes_ref),
        (edge_in_hbm, edge_in_ref),
        (edge_bias_hbm, edge_bias_ref),
        (node_in_hbm.at[0], node_in_ref),
        (node_bias_hbm, node_bias_ref),
        (pair_hbm, pair_ref),
        (quad_hbm, quads_ref),
        (top_hbm, tops_ref),
        (near_hbm.at[0, 0], near_rows),
    ):
        copy = pltpu.make_async_copy(source, target, load_sems.at[len(loads)])
        copy.start()
        loads.append(copy)

    slot_of = slots_ref[...]
    loads[0].wait()
    pl.semaphore_wait(barrier, owners - 1)

    def of_owner(owner):
        return pl.ds(pl.multiple_of(owner * cap, PAD), cap)

    def delivery(owner, sender):
        return pltpu.make_async_remote_copy(
            src_ref=placed.at[of_owner(owner), :],
            dst_ref=arrived.at[of_owner(sender), :],
            send_sem=place_sems.at[0, owner],
            recv_sem=place_sems.at[1, sender],
            device_id=mesh_place(owner),
            device_id_type=pl.DeviceIdType.MESH,
        )

    @pl.loop(0, tiles)
    def _(step):
        t = lax.rem(a + step, tiles)
        start = pl.multiple_of(t * tile, tile)
        weight = jnp.where(rows_of((tile, nodes), start) == slot_of, 1.0, 0.0)
        filled = jnp.max(weight, axis=1, keepdims=True)
        rows = dot(weight.astype(bf16), nodes_ref[...])
        placed[pl.ds(start, tile), :] = jnp.where(filled > 0.5, rows, EMPTY).astype(bf16)

        @pl.loop(0, per_tile)
        def _(k):
            owner = t * per_tile + k

            @pl.when(owner != me)
            def _():
                delivery(owner, me).start()

    arrived[of_owner(me), :] = placed[of_owner(me), :]

    for copy in loads[5:8]:
        copy.wait()
    quad_ref, top_ref = quads_ref.at[a // 2], tops_ref.at[a // 4]

    def compose(outer, inner_row, target_ref):
        which = rows_of((8, count))
        high = (outer >> 7).astype(f32)
        low = (outer & 127).astype(f32)
        parts[...] = jnp.where(which == 0, high, jnp.where(which == 1, low, 0.0))
        sums[...] = jnp.zeros_like(sums)

        @pl.loop(0, tiles)
        def _(t):
            start = pl.multiple_of(t * tile, tile)
            sel = one_hot(rows_of((tile, count), start) == inner_row)
            sums[...] += dot(parts[:, pl.ds(start, tile)].astype(bf16), sel)

        total = sums[...]
        target_ref[...] = (total[0:1] * 128.0 + total[1:2]).astype(jnp.int32)

    compose(pair_ref[...], quad_ref[...], two_ref)
    compose(two_ref[...], top_ref[...], three_ref)
    for copy in loads[1:5] + loads[8:]:
        copy.wait()
    near_count = near_ref.shape[1]

    @pl.loop(0, tiles)
    def _(t):
        start = pl.multiple_of(t * tile, tile)
        pair_hot[pl.ds(start, tile), :] = picker(pair_ref, start, tile, 0, count)

    @pl.loop(0, count // LANES)
    def _(t):
        here = pl.ds(pl.multiple_of(t * LANES, LANES), LANES)
        turned = jnp.concatenate([near_rows[:, here]] * (LANES // near_count), axis=0).T
        near_ref[here, :] = turned[:, 0:near_count]

    @pl.loop(0, tiles)
    def _(step):
        t = lax.rem(a - step + tiles * owners, tiles)

        @pl.loop(0, per_tile)
        def _(k):
            sender = t * per_tile + k

            @pl.when(sender != me)
            def _():
                delivery(me, sender).wait_recv()

        here = pl.ds(pl.multiple_of(t * tile, tile), tile)
        raw = arrived[here, :].astype(f32)
        present = raw[:, 0:1] < LIMIT
        rows = jnp.where(present, raw, 0.0).astype(bf16)
        to_dst = (dot(rows, edge_in_ref[0]) + edge_bias_ref[...]) * 0.5
        dst[here, :] = to_dst.astype(bf16)
        from_src = dot(rows, edge_in_ref[1]) * 0.5
        src[here, :] = jnp.where(present, from_src, AWAY).astype(bf16)
        raised[here, :] = dot(rows, node_in_ref[...]) + node_bias_ref[...]

    @pl.loop(0, owners)
    def _(owner):
        @pl.when(owner != me)
        def _():
            delivery(owner, me).wait_send()


def fine_kernel(
    tile_src_ref,
    arrived,
    dst,
    src,
    raised,
    near_ref,
    edge_out_hbm,
    node_in_hbm,
    node_out_hbm,
    gain_ref,
    fine_ref,
    edge_out_ref,
    node_in_ref,
    node_out_ref,
    agg,
    sels,
    weights,
    near_a,
    near_b,
    load_sems,
):
    count, features = fine_ref.shape
    tile = 256
    tiles = count // tile
    loads = []
    for source, target in (
        (edge_out_hbm, edge_out_ref),
        (node_in_hbm.at[1], node_in_ref),
        (node_out_hbm, node_out_ref),
    ):
        copy = pltpu.make_async_copy(source, target, load_sems.at[len(loads)])
        copy.start()
        loads.append(copy)

    many_near = 4
    pieces_near = TPB * NBR // many_near
    group = 32
    eye = one_hot(rows_of((BLK, BLK)) == lanes_of((BLK, BLK)))
    for p in range(2):
        for i in range(TPB * NBR):
            sels[p, i * BLK : (i + 1) * BLK, BLK : 2 * BLK] = eye

    def gather(b, p, near, i):
        start = pl.multiple_of(b * BLK, BLK)
        j = i * many_near // NBR
        if i * many_near % NBR == 0:
            first = pl.multiple_of(tile_src_ref[0, 0, j, b] * BLK, BLK)
            weights[p, j, 0:BLK, :] = src[pl.ds(first, BLK), :]
            weights[p, j, BLK : 2 * BLK, :] = dst[pl.ds(start, BLK), :]
        which = near_ref[pl.ds(start, BLK), :]
        for k in range(i * many_near, (i + 1) * many_near):
            mask = which[:, k : k + 1] == lanes_of((BLK, BLK))
            sels[p, k * BLK : (k + 1) * BLK, 0:BLK] = one_hot(mask)
        rows = slice(i * many_near * BLK, (i + 1) * many_near * BLK)
        near[rows, :] = dot(sels[p, rows, :], weights[p, j]).astype(bf16)

    def settle(b, near, r):
        total = jnp.zeros((group, features), f32)
        for k in range(0, TPB * NBR, 4):
            terms = [
                half_silu(near[at * BLK + r : at * BLK + r + group, :]) for at in range(k, k + 4)
            ]
            total += ((terms[0] + terms[1]) + (terms[2] + terms[3])).astype(f32)
        agg[pl.ds(pl.multiple_of(b * BLK, BLK) + r, group), :] = total.astype(bf16)

    def both(ahead, p, near_next, b, near):
        sums = BLK // group
        for i in range(max(pieces_near, sums)):
            if i * pieces_near % max(pieces_near, sums) == 0:
                gather(ahead, p, near_next, i * pieces_near // max(pieces_near, sums))
            if i * sums % max(pieces_near, sums) == 0:
                settle(b, near, i * sums // max(pieces_near, sums) * group)

    for i in range(pieces_near):
        gather(0, 0, near_a, i)
    blocks = count // BLK

    @pl.loop(0, blocks // 2)
    def _(h):
        b = 2 * h
        both(b + 1, 1, near_b, b, near_a)
        both(lax.rem(b + 2, blocks), 0, near_a, b + 1, near_b)

    for copy in loads:
        copy.wait()

    many = 1024

    @pl.loop(0, count // many)
    def _(t):
        here = pl.ds(pl.multiple_of(t * many, many), many)
        message = dot(agg[here, :], edge_out_ref[...]).astype(bf16)
        lifted = raised[here, :] + dot(message, node_in_ref[...])
        hidden = half_silu(lifted * 0.5).astype(bf16)
        delta = dot(hidden, node_out_ref[...])
        scale = lax.rsqrt(jnp.mean(delta * delta, axis=-1, keepdims=True) + epsilon)
        raw = arrived[here, :].astype(f32)
        fine = raw + gain_ref[...] * (delta * scale)
        fine_ref[here, :] = jnp.where(raw[:, 0:1] < LIMIT, fine, EMPTY).astype(bf16)


def tree_kernel(
    groups,
    fine_ref,
    pair_ref,
    pair_hot,
    quads_ref,
    tops_ref,
    two_ref,
    three_ref,
    coarse_ref,
    out_ref,
    side,
    partner,
    level_one,
    wide_one,
    mine,
    theirs,
    my_marks,
    their_marks,
    wide_two,
    packets,
    inbox,
    packet_marks,
    inbox_marks,
    level_three,
    raised,
    top_hot,
    side_sems,
    quad_sems,
    quad_mark_sems,
    two_sems,
    group_sems,
    group_mark_sems,
    spread_sems,
):
    count, features = fine_ref.shape
    half, quarter = count // 2, count // 4
    piece = quarter // groups
    tile, big = 256, 512
    a, g = lax.axis_index("sub"), lax.axis_index("grp")
    quad_ref, top_ref = quads_ref.at[a // 2], tops_ref.at[a // 4]
    core = a + 1 - 2 * (a % 2)
    across = a + 2 - 4 * ((a // 2) % 2)
    others = [lax.rem(g + d, groups) for d in range(1, groups)]
    peers = [{"grp": t} for t in others] + [{"sub": across}, {"sub": core}]
    barrier = pltpu.get_barrier_semaphore()
    for peer in peers:
        pl.semaphore_signal(barrier, inc=1, device_id=peer, device_id_type=pl.DeviceIdType.MESH)

    def send(sems, at, source, target, peer):
        copy = pltpu.make_async_remote_copy(
            src_ref=source,
            dst_ref=target,
            send_sem=sems.at[(0, *at)],
            recv_sem=sems.at[(1, *at)],
            device_id=peer,
            device_id_type=pl.DeviceIdType.MESH,
        )
        copy.start()
        return copy

    many = 1024
    sides = []
    for t in range(count // many):
        here = pl.ds(t * many, many)
        side[here, :] = dot(pair_hot[here, :], fine_ref[...]).astype(bf16)
        if t == 0:
            pl.semaphore_wait(barrier, len(peers))
        sides.append(send(side_sems, (t,), side.at[here, :], partner.at[here, :], {"sub": core}))
    for t in range(count // many):
        sides[t].wait_recv()
        for start in range(t * many, (t + 1) * many, big):
            here = pl.ds(start, big)
            x = side[here, :].astype(f32)
            y = partner[here, :].astype(f32)
            in_x = x[:, 0:1] < LIMIT
            in_y = y[:, 0:1] < LIMIT
            total = jnp.where(in_x, x, 0.0) + jnp.where(in_y, y, 0.0)
            marks = jnp.where(in_x, 1.0, 0.0) + jnp.where(in_y, 1.0, 0.0)
            level = refined(total, marks, coarse_ref[0]).astype(bf16)
            level_one[here, :] = level
            wide_one[here, 0:features] = level
            wide_one[here, features : features + LANES] = jnp.broadcast_to(
                marks, (big, LANES)
            ).astype(bf16)

    quads, quad_marks = [], []
    for t in range(half // tile):
        sel = picker(quad_ref, (a % 2) * half + t * tile, tile, 0, count)
        got = dot(sel, wide_one[...])
        columns = [got[c : c + LANES, features : features + LANES] for c in range(0, tile, LANES)]
        put_marks(my_marks, t, columns)
        quad_marks.append(
            send(quad_mark_sems, (t,), my_marks.at[t], their_marks.at[t], {"sub": across})
        )
        here = pl.ds(t * tile, tile)
        mine[here, :] = got[:, 0:features].astype(bf16)
        quads.append(send(quad_sems, (t,), mine.at[here, :], theirs.at[here, :], {"sub": across}))

    @pl.loop(0, count // big)
    def _(t):
        start = pl.multiple_of(t * big, big)
        here = pl.ds(start, big)
        sel = one_hot(rows_of((big, count), start) == pair_ref[...])
        raised[here, :] = fine_ref[here, :].astype(f32) + dot(sel, level_one[...])

    top_hot[...] = picker(top_ref, (a % 4) * quarter, quarter, 0, count)
    base = pl.multiple_of((a % 2) * half, half)
    twos = []
    for t in range(half // tile):
        quads[t].wait_recv()
        quad_marks[t].wait_recv()
        for c in range(0, tile, LANES):
            line = c // LANES
            x = spread(my_marks[t, line : line + 1, :])
            y = spread(their_marks[t, line : line + 1, :])
            at = t * tile + c
            total = widened(x, features) * mine[at : at + LANES, :].astype(f32) + widened(
                y, features
            ) * theirs[at : at + LANES, :].astype(f32)
            level = refined(total, widened(x + y, features), coarse_ref[1])
            there = pl.ds(base + t * tile + c, LANES)
            wide_two[there, 0:features] = level.astype(bf16)
            wide_two[there, features : features + LANES] = (x + y).astype(bf16)
        there = wide_two.at[pl.ds(base + t * tile, tile), :]
        twos.append(send(two_sems, (t,), there, there, {"sub": core}))
    for copy in twos:
        copy.wait_recv()

    got = dot(top_hot[...], wide_two[...])
    for t in range(groups):
        at = t * piece
        packets[at : at + piece, :] = got[at : at + piece, 0:features].astype(bf16)
        columns = [
            got[at + c : at + c + LANES, features : features + LANES]
            for c in range(0, piece, LANES)
        ]
        put_marks(packet_marks, t, columns)
    parcels = []
    for d, t in enumerate(others):
        here = pl.ds(pl.multiple_of(t * piece, piece), piece)
        peer = {"grp": t}
        parcels.append(
            send(group_mark_sems, (d,), packet_marks.at[t], inbox_marks.at[d], peer)
        )
        parcels.append(send(group_sems, (d,), packets.at[here, :], inbox.at[d], peer))

    @pl.loop(0, count // big)
    def _(t):
        start = pl.multiple_of(t * big, big)
        here = pl.ds(start, big)
        sel = one_hot(rows_of((big, count), start) == two_ref[...])
        raised[here, :] += dot(sel, wide_two[:, 0:features])

    for copy in parcels:
        copy.wait_recv()
    own = pl.multiple_of(g * piece, piece)
    terms = [lambda c: packets[pl.ds(own + c, LANES), :].astype(f32)]
    marked = [lambda line: packet_marks[g, line : line + 1, :]]
    for d in range(groups - 1):
        terms.append(lambda c, d=d: inbox[d, c : c + LANES, :].astype(f32))
        marked.append(lambda line, d=d: inbox_marks[d, line : line + 1, :])

    def piece_of(sub, group):
        return pl.ds(pl.multiple_of((group * 4 + sub % 4) * piece, piece), piece)

    base_three = pl.multiple_of((g * 4 + a % 4) * piece, piece)
    for c in range(0, piece, LANES):
        total, marks = 0.0, 0.0
        for term, marked_by in zip(terms, marked):
            got = spread(marked_by(c // LANES))
            marks = marks + got
            total = total + widened(got, features) * term(c)
        level = refined(total, widened(marks, features), coarse_ref[2])
        level_three[pl.ds(base_three + c, LANES), :] = level.astype(bf16)

    near = g + 1 - 2 * (g % 2)
    order = [g, near, 2 - g // 2, 3 - 3 * (g // 2)]

    def relay(stage, leaves, comes, rows, peer):
        there = level_three.at[rows, :]
        return pltpu.make_async_remote_copy(
            src_ref=there,
            dst_ref=there,
            send_sem=spread_sems.at[0, stage, leaves],
            recv_sem=spread_sems.at[1, stage, comes],
            device_id=peer,
            device_id_type=pl.DeviceIdType.MESH,
        )

    def lift(group, sub, subs, last):
        targets = jnp.concatenate(
            [
                three_ref[:, pl.ds(pl.multiple_of((i * groups + group) * piece, piece), piece)]
                for i in [sub + j for j in range(subs)]
            ],
            axis=1,
        )
        width = subs * piece
        rows = pl.ds(pl.multiple_of((group * 4 + sub) * piece, piece), width)

        @pl.loop(0, count // big)
        def _(t):
            start = pl.multiple_of(t * big, big)
            here = pl.ds(start, big)
            sel = one_hot(rows_of((big, width), start) == targets)
            total = raised[here, :] + dot(sel, level_three[rows, :])
            if last:
                present = fine_ref[here, 0:LANES].astype(f32)[:, 0:1] < LIMIT
                out_ref[here, :] = jnp.where(present, total, 0.0).astype(bf16)
            else:
                raised[here, :] = total

    over_x, over_core, relayed = [], [], []

    def pass_on(group):
        over_x.append(relay(1, group, group, piece_of(a, group), {"sub": across}))
        over_x[-1].start()
        over_core.append(relay(2, group, group, piece_of(a, group), {"sub": core}))
        over_core[-1].start()

    def finish(k, last):
        group = order[k]
        over_x[k].wait_recv()
        relayed.append(relay(3, group, group, piece_of(across, group), {"sub": core}))
        relayed[k].start()
        over_core[k].wait_recv()
        if last:
            pair = (a % 4) // 2 * 2
            lift(group, pair, 2, False)
            relayed[k].wait_recv()
            lift(group, 2 - pair, 2, True)
        else:
            relayed[k].wait_recv()
            lift(group, 0, 4, False)

    mine_at = piece_of(a, g)
    pass_on(g)
    over_z = [relay(0, t, g, mine_at, {"grp": t}) for t in order[1:3]]
    for copy in over_z:
        copy.start()
    inner = g % 3 != 0
    mid, far = order[2:]

    def arrival(source):
        return relay(0, source, source, piece_of(a, source), {"grp": source})

    def hop(source):
        there = level_three.at[piece_of(a, source), :]
        return pltpu.make_async_remote_copy(
            src_ref=there,
            dst_ref=there,
            send_sem=spread_sems.at[0, 4, source],
            recv_sem=spread_sems.at[1, 0, source],
            device_id={"grp": near},
            device_id_type=pl.DeviceIdType.MESH,
        )

    arrival(near).wait_recv()
    pass_on(near)
    for k, source in ((0, mid), (1, far)):

        @pl.when(inner)
        def _():
            arrival(source).wait_recv()
            hop(source).start()

        finish(k, False)

        @pl.when(jnp.logical_not(inner))
        def _():
            arrival(source).wait_recv()

        pass_on(source)
    finish(2, False)
    finish(3, True)

    @pl.when(inner)
    def _():
        hop(mid).wait_send()
        hop(far).wait_send()

    for copy in sides + quads + quad_marks + twos + parcels + over_z + over_x + over_core + relayed:
        copy.wait_send()


def body(
    node_rows,
    owners,
    tile_src,
    neighbors,
    pool_pair,
    pool_quad,
    pool_top,
    edge_in,
    edge_bias,
    edge_out,
    node_in,
    node_bias,
    node_out,
    out_gain,
    coarse,
):
    groups = lax.axis_size("grp")
    owner_count = lax.axis_size("sub") * groups
    count, near_count = neighbors.shape[2:]
    nodes, features = node_rows.shape
    cap = count // owner_count
    half, quarter = count // 2, count // 4
    piece = quarter // groups
    tile = 256

    def shape(rows, dtype=bf16, width=features):
        return jax.ShapeDtypeStruct((rows, width), dtype)

    def room(like):
        return pltpu.VMEM(like.shape, like.dtype)

    pair = pool_pair.reshape(1, count)
    edge_row, node_row = edge_bias.reshape(1, features), node_bias.reshape(1, features)
    rows = pltpu.VMEM((count, features), bf16)
    sums = pltpu.VMEM((8, count), f32)
    square = pltpu.VMEM((features, features), bf16)
    slots = pl.pallas_call(
        functools.partial(slot_kernel, cap),
        out_shape=shape(1, jnp.int32, nodes),
        in_specs=[VM],
        out_specs=VM,
        compiler_params=pltpu.CompilerParams(vmem_limit_bytes=8 << 20),
        cost_estimate=pl.CostEstimate(
            flops=20 * 10**9, bytes_accessed=8 << 20, transcendentals=0
        ),
    )(owners.reshape(1, nodes))
    arrived, dst, src, lifted, near, to_two, to_three, pair_hot = pl.pallas_call(
        functools.partial(owner_kernel, groups, cap),
        out_shape=(
            shape(count),
            shape(count),
            shape(count),
            shape(count, f32),
            jax.ShapeDtypeStruct(neighbors.shape[2:], jnp.int32),
            shape(1, jnp.int32, count),
            shape(1, jnp.int32, count),
            shape(count, bf16, count),
        ),
        in_specs=[VM] + [HB] * 9,
        out_specs=(VM,) * 8,
        scratch_shapes=[
            room(node_rows),
            pltpu.VMEM((near_count, count), jnp.int32),
            room(pair),
            room(pool_quad),
            room(pool_top),
            room(edge_in),
            room(edge_row),
            square,
            room(node_row),
            sums,
            sums,
            rows,
            pltpu.SemaphoreType.DMA((9,)),
            pltpu.SemaphoreType.DMA((2, owner_count)),
        ],
        compiler_params=pltpu.CompilerParams(
            collective_id=1, has_side_effects=True, vmem_limit_bytes=24 << 20
        ),
    )(
        slots,
        node_rows,
        jnp.swapaxes(neighbors, 2, 3),
        pair,
        pool_quad,
        pool_top,
        edge_in,
        edge_row,
        node_in,
        node_row,
    )
    gathered = pltpu.VMEM((TPB * NBR * BLK, features), bf16)
    fine = pl.pallas_call(
        fine_kernel,
        out_shape=shape(count),
        in_specs=[SM] + [VM] * 5 + [HB] * 3 + [VM],
        out_specs=VM,
        scratch_shapes=[square] * 3
        + [
            rows,
            pltpu.VMEM((2, TPB * NBR * BLK, 2 * BLK), bf16),
            pltpu.VMEM((2, TPB, 2 * BLK, features), bf16),
            gathered,
            gathered,
            pltpu.SemaphoreType.DMA((3,)),
        ],
        compiler_params=pltpu.CompilerParams(vmem_limit_bytes=28 << 20),
        cost_estimate=pl.CostEstimate(
            flops=20 * 10**9, bytes_accessed=8 << 20, transcendentals=0
        ),
    )(
        jnp.swapaxes(tile_src, 2, 3),
        arrived,
        dst,
        src,
        lifted,
        near,
        edge_out,
        node_in,
        node_out,
        out_gain.reshape(1, features),
    )
    wide = pltpu.VMEM((count, features + LANES), bf16)
    pooled = pltpu.VMEM((half, features), bf16)
    marks = pltpu.VMEM((half // tile, MARKS, LANES), f32)
    return pl.pallas_call(
        functools.partial(tree_kernel, groups),
        out_shape=shape(count),
        in_specs=[VM] * 8,
        out_specs=VM,
        scratch_shapes=[
            rows,
            rows,
            rows,
            wide,
            pooled,
            pooled,
            marks,
            marks,
            wide,
            pltpu.VMEM((groups * piece, features), bf16),
            pltpu.VMEM((groups - 1, piece, features), bf16),
            pltpu.VMEM((groups, MARKS, LANES), f32),
            pltpu.VMEM((groups - 1, MARKS, LANES), f32),
            rows,
            pltpu.VMEM((count, features), f32),
            pltpu.VMEM((quarter, count), bf16),
            pltpu.SemaphoreType.DMA((2, count // 1024)),
            pltpu.SemaphoreType.DMA((2, half // tile)),
            pltpu.SemaphoreType.DMA((2, half // tile)),
            pltpu.SemaphoreType.DMA((2, half // tile)),
            pltpu.SemaphoreType.DMA((2, groups)),
            pltpu.SemaphoreType.DMA((2, groups)),
            pltpu.SemaphoreType.DMA((2, 5, groups)),
        ],
        compiler_params=pltpu.CompilerParams(
            collective_id=0, has_side_effects=True, vmem_limit_bytes=40 << 20
        ),
    )(fine, pair, pair_hot, pool_quad, pool_top, to_two, to_three, coarse)


def solution(mesh):
    in_specs = (
        P(("sub", "grp"), None),
        P(("sub", "grp")),
        P("sub", "grp", None, None),
        P("sub", "grp", None, None),
        P("sub", "grp", None),
        P(None, "grp", None),
        P(None, "grp", None),
        P(),
        P(),
        P(),
        P(),
        P(),
        P(),
        P(),
        P(),
    )
    out_specs = P(("sub", "grp"), None)
    return jax.shard_map(body, mesh=mesh, in_specs=in_specs, out_specs=out_specs, check_vma=False)
```

```python
import functools

import jax
import jax.numpy as jnp
from jax import lax
from jax.experimental import pallas as pl
from jax.experimental.pallas import tpu as pltpu
from jax.sharding import PartitionSpec as P

BLK = 128
TPB = 2
NBR = 8
LANES = 128
PAD = 16
MARKS = 8
EMPTY = 16384.0
LIMIT = 8192.0
AWAY = -8192.0
epsilon = 1e-05
f32 = jnp.float32
bf16 = jnp.bfloat16

VM = pl.BlockSpec(memory_space=pltpu.VMEM)
SM = pl.BlockSpec(memory_space=pltpu.SMEM)
HB = pl.BlockSpec(memory_space=pltpu.HBM)


def rows_of(shape, start=0):
    return lax.broadcasted_iota(jnp.int32, shape, 0) + start


def lanes_of(shape, start=0):
    return lax.broadcasted_iota(jnp.int32, shape, 1) + start


def one_hot(mask):
    return jnp.where(mask, 1.0, 0.0).astype(bf16)


def spread(row):
    return jnp.broadcast_to(row, (LANES, LANES)).T


def dot(a, b):
    return jnp.dot(a, b, preferred_element_type=f32)


def half_silu(h):
    return h + h * jnp.tanh(h)


def picker(perm_ref, first, count, start, width):
    tiles = []
    for c in range(0, count, LANES):
        column = spread(perm_ref[:, pl.ds(pl.multiple_of(first + c, LANES), LANES)])
        wide = jnp.concatenate([column] * (width // LANES), axis=1)
        tiles.append(one_hot(wide == lanes_of((LANES, width), start)))
    return jnp.concatenate(tiles, axis=0)


def refined(total, count, weight):
    mean_rows = total * (1.0 / jnp.maximum(count, 1.0))
    lifted = dot(mean_rows.astype(bf16), weight)
    return mean_rows + half_silu(lifted * 0.5)


def widened(column, features):
    return jnp.concatenate([column] * (features // LANES), axis=1)


def put_marks(out_ref, at, columns):
    lines = [col.T[0:1, :] for col in columns]
    lines.append(jnp.zeros((MARKS - len(lines), LANES), f32))
    out_ref[at] = jnp.concatenate(lines, axis=0)


def slot_kernel(cap, owners_ref, slots_ref):
    nodes = owners_ref.shape[1]
    owner_row = owners_ref[...]
    position = jnp.zeros((1, nodes), f32)
    for c in range(0, nodes, LANES):
        column = spread(owners_ref[:, c : c + LANES])
        wide = jnp.concatenate([column] * (nodes // LANES), axis=1)
        shape = (LANES, nodes)
        earlier = (wide == owner_row) & (rows_of(shape, c) < lanes_of(shape))
        position += jnp.sum(jnp.where(earlier, 1.0, 0.0), axis=0, keepdims=True)
    slots_ref[...] = owner_row * cap + position.astype(jnp.int32)


def owner_kernel(
    groups,
    cap,
    slots_ref,
    node_rows_hbm,
    near_hbm,
    pair_hbm,
    quad_hbm,
    top_hbm,
    edge_in_hbm,
    edge_bias_hbm,
    node_in_hbm,
    node_bias_hbm,
    arrived,
    dst,
    src,
    raised,
    near_ref,
    two_ref,
    three_ref,
    pair_hot,
    nodes_ref,
    near_rows,
    pair_ref,
    quads_ref,
    tops_ref,
    edge_in_ref,
    edge_bias_ref,
    node_in_ref,
    node_bias_ref,
    parts,
    sums,
    placed,
    load_sems,
    place_sems,
):
    count, features = arrived.shape
    nodes = nodes_ref.shape[0]
    tile = 256
    a, g = lax.axis_index("sub"), lax.axis_index("grp")
    me = a * groups + g
    owners = count // cap
    per_tile = tile // cap
    tiles = count // tile

    def mesh_place(owner):
        return {"sub": owner // groups, "grp": owner % groups}

    barrier = pltpu.get_barrier_semaphore()

    @pl.loop(0, owners)
    def _(owner):
        @pl.when(owner != me)
        def _():
            pl.semaphore_signal(
                barrier,
                inc=1,
                device_id=mesh_place(owner),
                device_id_type=pl.DeviceIdType.MESH,
            )

    loads = []
    for source, target in (
        (node_rows_hbm, nodes_ref),
        (edge_in_hbm, edge_in_ref),
        (edge_bias_hbm, edge_bias_ref),
        (node_in_hbm.at[0], node_in_ref),
        (node_bias_hbm, node_bias_ref),
        (pair_hbm, pair_ref),
        (quad_hbm, quads_ref),
        (top_hbm, tops_ref),
        (near_hbm.at[0, 0], near_rows),
    ):
        copy = pltpu.make_async_copy(source, target, load_sems.at[len(loads)])
        copy.start()
        loads.append(copy)

    slot_of = slots_ref[...]
    loads[0].wait()
    pl.semaphore_wait(barrier, owners - 1)

    def of_owner(owner):
        return pl.ds(pl.multiple_of(owner * cap, PAD), cap)

    def delivery(owner, sender):
        return pltpu.make_async_remote_copy(
            src_ref=placed.at[of_owner(owner), :],
            dst_ref=arrived.at[of_owner(sender), :],
            send_sem=place_sems.at[0, owner],
            recv_sem=place_sems.at[1, sender],
            device_id=mesh_place(owner),
            device_id_type=pl.DeviceIdType.MESH,
        )

    @pl.loop(0, tiles)
    def _(step):
        t = lax.rem(a + step, tiles)
        start = pl.multiple_of(t * tile, tile)
        weight = jnp.where(rows_of((tile, nodes), start) == slot_of, 1.0, 0.0)
        filled = jnp.max(weight, axis=1, keepdims=True)
        rows = dot(weight.astype(bf16), nodes_ref[...])
        placed[pl.ds(start, tile), :] = jnp.where(filled > 0.5, rows, EMPTY).astype(bf16)

        @pl.loop(0, per_tile)
        def _(k):
            owner = t * per_tile + k

            @pl.when(owner != me)
            def _():
                delivery(owner, me).start()

    arrived[of_owner(me), :] = placed[of_owner(me), :]

    for copy in loads[5:8]:
        copy.wait()
    quad_ref, top_ref = quads_ref.at[a // 2], tops_ref.at[a // 4]

    def compose(outer, inner_row, target_ref):
        which = rows_of((8, count))
        high = (outer >> 7).astype(f32)
        low = (outer & 127).astype(f32)
        parts[...] = jnp.where(which == 0, high, jnp.where(which == 1, low, 0.0))
        sums[...] = jnp.zeros_like(sums)

        @pl.loop(0, tiles)
        def _(t):
            start = pl.multiple_of(t * tile, tile)
            sel = one_hot(rows_of((tile, count), start) == inner_row)
            sums[...] += dot(parts[:, pl.ds(start, tile)].astype(bf16), sel)

        total = sums[...]
        target_ref[...] = (total[0:1] * 128.0 + total[1:2]).astype(jnp.int32)

    compose(pair_ref[...], quad_ref[...], two_ref)
    compose(two_ref[...], top_ref[...], three_ref)
    for copy in loads[1:5] + loads[8:]:
        copy.wait()
    near_count = near_ref.shape[1]

    @pl.loop(0, tiles)
    def _(t):
        start = pl.multiple_of(t * tile, tile)
        pair_hot[pl.ds(start, tile), :] = picker(pair_ref, start, tile, 0, count)

    @pl.loop(0, count // LANES)
    def _(t):
        here = pl.ds(pl.multiple_of(t * LANES, LANES), LANES)
        turned = jnp.concatenate([near_rows[:, here]] * (LANES // near_count), axis=0).T
        near_ref[here, :] = turned[:, 0:near_count]

    @pl.loop(0, tiles)
    def _(step):
        t = lax.rem(a - step + tiles * owners, tiles)

        @pl.loop(0, per_tile)
        def _(k):
            sender = t * per_tile + k

            @pl.when(sender != me)
            def _():
                delivery(me, sender).wait_recv()

        here = pl.ds(pl.multiple_of(t * tile, tile), tile)
        raw = arrived[here, :].astype(f32)
        present = raw[:, 0:1] < LIMIT
        rows = jnp.where(present, raw, 0.0).astype(bf16)
        to_dst = (dot(rows, edge_in_ref[0]) + edge_bias_ref[...]) * 0.5
        dst[here, :] = to_dst.astype(bf16)
        from_src = dot(rows, edge_in_ref[1]) * 0.5
        src[here, :] = jnp.where(present, from_src, AWAY).astype(bf16)
        raised[here, :] = dot(rows, node_in_ref[...]) + node_bias_ref[...]

    @pl.loop(0, owners)
    def _(owner):
        @pl.when(owner != me)
        def _():
            delivery(owner, me).wait_send()


def fine_kernel(
    tile_src_ref,
    arrived,
    dst,
    src,
    raised,
    near_ref,
    edge_out_hbm,
    node_in_hbm,
    node_out_hbm,
    gain_ref,
    fine_ref,
    edge_out_ref,
    node_in_ref,
    node_out_ref,
    agg,
    sels,
    weights,
    near_a,
    near_b,
    load_sems,
):
    count, features = fine_ref.shape
    tile = 256
    tiles = count // tile
    loads = []
    for source, target in (
        (edge_out_hbm, edge_out_ref),
        (node_in_hbm.at[1], node_in_ref),
        (node_out_hbm, node_out_ref),
    ):
        copy = pltpu.make_async_copy(source, target, load_sems.at[len(loads)])
        copy.start()
        loads.append(copy)

    many_near = 4
    pieces_near = TPB * NBR // many_near
    group = 32
    eye = one_hot(rows_of((BLK, BLK)) == lanes_of((BLK, BLK)))
    for p in range(2):
        for i in range(TPB * NBR):
            sels[p, i * BLK : (i + 1) * BLK, BLK : 2 * BLK] = eye

    def gather(b, p, near, i):
        start = pl.multiple_of(b * BLK, BLK)
        j = i * many_near // NBR
        if i * many_near % NBR == 0:
            first = pl.multiple_of(tile_src_ref[0, 0, j, b] * BLK, BLK)
            weights[p, j, 0:BLK, :] = src[pl.ds(first, BLK), :]
            weights[p, j, BLK : 2 * BLK, :] = dst[pl.ds(start, BLK), :]
        which = near_ref[pl.ds(start, BLK), :]
        for k in range(i * many_near, (i + 1) * many_near):
            mask = which[:, k : k + 1] == lanes_of((BLK, BLK))
            sels[p, k * BLK : (k + 1) * BLK, 0:BLK] = one_hot(mask)
        rows = slice(i * many_near * BLK, (i + 1) * many_near * BLK)
        near[rows, :] = dot(sels[p, rows, :], weights[p, j]).astype(bf16)

    def settle(b, near, r):
        total = jnp.zeros((group, features), f32)
        for k in range(0, TPB * NBR, 4):
            terms = [
                half_silu(near[at * BLK + r : at * BLK + r + group, :]) for at in range(k, k + 4)
            ]
            total += ((terms[0] + terms[1]) + (terms[2] + terms[3])).astype(f32)
        agg[pl.ds(pl.multiple_of(b * BLK, BLK) + r, group), :] = total.astype(bf16)

    def both(ahead, p, near_next, b, near):
        sums = BLK // group
        for i in range(max(pieces_near, sums)):
            if i * pieces_near % max(pieces_near, sums) == 0:
                gather(ahead, p, near_next, i * pieces_near // max(pieces_near, sums))
            if i * sums % max(pieces_near, sums) == 0:
                settle(b, near, i * sums // max(pieces_near, sums) * group)

    for i in range(pieces_near):
        gather(0, 0, near_a, i)
    blocks = count // BLK

    @pl.loop(0, blocks // 2)
    def _(h):
        b = 2 * h
        both(b + 1, 1, near_b, b, near_a)
        both(lax.rem(b + 2, blocks), 0, near_a, b + 1, near_b)

    for copy in loads:
        copy.wait()

    many = 1024

    @pl.loop(0, count // many)
    def _(t):
        here = pl.ds(pl.multiple_of(t * many, many), many)
        message = dot(agg[here, :], edge_out_ref[...]).astype(bf16)
        lifted = raised[here, :] + dot(message, node_in_ref[...])
        hidden = half_silu(lifted * 0.5).astype(bf16)
        delta = dot(hidden, node_out_ref[...])
        scale = lax.rsqrt(jnp.mean(delta * delta, axis=-1, keepdims=True) + epsilon)
        raw = arrived[here, :].astype(f32)
        fine = raw + gain_ref[...] * (delta * scale)
        fine_ref[here, :] = jnp.where(raw[:, 0:1] < LIMIT, fine, EMPTY).astype(bf16)


def tree_kernel(
    groups,
    fine_ref,
    pair_ref,
    pair_hot,
    quads_ref,
    tops_ref,
    two_ref,
    three_ref,
    coarse_ref,
    out_ref,
    side,
    partner,
    level_one,
    wide_one,
    mine,
    theirs,
    my_marks,
    their_marks,
    wide_two,
    packets,
    inbox,
    packet_marks,
    inbox_marks,
    level_three,
    raised,
    top_hot,
    picked,
    last_hot,
    side_sems,
    quad_sems,
    quad_mark_sems,
    two_sems,
    group_sems,
    group_mark_sems,
    spread_sems,
):
    count, features = fine_ref.shape
    half, quarter = count // 2, count // 4
    piece = quarter // groups
    tile, big = 256, 512
    a, g = lax.axis_index("sub"), lax.axis_index("grp")
    quad_ref, top_ref = quads_ref.at[a // 2], tops_ref.at[a // 4]
    core = a + 1 - 2 * (a % 2)
    across = a + 2 - 4 * ((a // 2) % 2)
    others = [lax.rem(g + d, groups) for d in range(1, groups)]
    peers = [{"grp": t} for t in others] + [{"sub": across}, {"sub": core}]
    barrier = pltpu.get_barrier_semaphore()
    for peer in peers:
        pl.semaphore_signal(barrier, inc=1, device_id=peer, device_id_type=pl.DeviceIdType.MESH)

    def send(sems, at, source, target, peer):
        copy = pltpu.make_async_remote_copy(
            src_ref=source,
            dst_ref=target,
            send_sem=sems.at[(0, *at)],
            recv_sem=sems.at[(1, *at)],
            device_id=peer,
            device_id_type=pl.DeviceIdType.MESH,
        )
        copy.start()
        return copy

    many = 1024
    sides = []
    for t in range(count // many):
        here = pl.ds(t * many, many)
        side[here, :] = dot(pair_hot[here, :], fine_ref[...]).astype(bf16)
        if t == 0:
            pl.semaphore_wait(barrier, len(peers))
        sides.append(send(side_sems, (t,), side.at[here, :], partner.at[here, :], {"sub": core}))
    for t in range(count // many):
        sides[t].wait_recv()
        for start in range(t * many, (t + 1) * many, big):
            here = pl.ds(start, big)
            x = side[here, :].astype(f32)
            y = partner[here, :].astype(f32)
            in_x = x[:, 0:1] < LIMIT
            in_y = y[:, 0:1] < LIMIT
            total = jnp.where(in_x, x, 0.0) + jnp.where(in_y, y, 0.0)
            marks = jnp.where(in_x, 1.0, 0.0) + jnp.where(in_y, 1.0, 0.0)
            level = refined(total, marks, coarse_ref[0]).astype(bf16)
            level_one[here, :] = level
            wide_one[here, 0:features] = level
            wide_one[here, features : features + LANES] = jnp.broadcast_to(
                marks, (big, LANES)
            ).astype(bf16)

    quads, quad_marks = [], []
    for t in range(half // tile):
        sel = picker(quad_ref, (a % 2) * half + t * tile, tile, 0, count)
        got = dot(sel, wide_one[...])
        columns = [got[c : c + LANES, features : features + LANES] for c in range(0, tile, LANES)]
        put_marks(my_marks, t, columns)
        quad_marks.append(
            send(quad_mark_sems, (t,), my_marks.at[t], their_marks.at[t], {"sub": across})
        )
        here = pl.ds(t * tile, tile)
        mine[here, :] = got[:, 0:features].astype(bf16)
        quads.append(send(quad_sems, (t,), mine.at[here, :], theirs.at[here, :], {"sub": across}))

    @pl.loop(0, count // big)
    def _(t):
        start = pl.multiple_of(t * big, big)
        here = pl.ds(start, big)
        sel = one_hot(rows_of((big, count), start) == pair_ref[...])
        raised[here, :] = fine_ref[here, :].astype(f32) + dot(sel, level_one[...])

    top_hot[...] = picker(top_ref, (a % 4) * quarter, quarter, 0, count)
    base = pl.multiple_of((a % 2) * half, half)
    twos = []
    for t in range(half // tile):
        quads[t].wait_recv()
        quad_marks[t].wait_recv()
        for c in range(0, tile, LANES):
            line = c // LANES
            x = spread(my_marks[t, line : line + 1, :])
            y = spread(their_marks[t, line : line + 1, :])
            at = t * tile + c
            total = widened(x, features) * mine[at : at + LANES, :].astype(f32) + widened(
                y, features
            ) * theirs[at : at + LANES, :].astype(f32)
            level = refined(total, widened(x + y, features), coarse_ref[1])
            there = pl.ds(base + t * tile + c, LANES)
            wide_two[there, 0:features] = level.astype(bf16)
            wide_two[there, features : features + LANES] = (x + y).astype(bf16)
        there = wide_two.at[pl.ds(base + t * tile, tile), :]
        twos.append(send(two_sems, (t,), there, there, {"sub": core}))
        mine_here = pl.ds(pl.multiple_of(base + t * tile, tile), tile)
        part = dot(top_hot[:, mine_here], wide_two[mine_here, :])
        twos[t].wait_recv()
        their_here = pl.ds(pl.multiple_of(half - base + t * tile, tile), tile)
        part += dot(top_hot[:, their_here], wide_two[their_here, :])
        if t == 0:
            picked[...] = part
        else:
            picked[...] += part

    got = picked[...]
    for t in range(groups):
        at = t * piece
        packets[at : at + piece, :] = got[at : at + piece, 0:features].astype(bf16)
        columns = [
            got[at + c : at + c + LANES, features : features + LANES]
            for c in range(0, piece, LANES)
        ]
        put_marks(packet_marks, t, columns)
    parcels = []
    for d, t in enumerate(others):
        here = pl.ds(pl.multiple_of(t * piece, piece), piece)
        peer = {"grp": t}
        parcels.append(
            send(group_mark_sems, (d,), packet_marks.at[t], inbox_marks.at[d], peer)
        )
        parcels.append(send(group_sems, (d,), packets.at[here, :], inbox.at[d], peer))

    @pl.loop(0, count // big)
    def _(t):
        start = pl.multiple_of(t * big, big)
        here = pl.ds(start, big)
        sel = one_hot(rows_of((big, count), start) == two_ref[...])
        raised[here, :] += dot(sel, wide_two[:, 0:features])

    near = g + 1 - 2 * (g % 2)
    order = [g, near, 2 - g // 2, 3 - 3 * (g // 2)]

    def targets_of(group, sub, subs):
        return jnp.concatenate(
            [
                three_ref[:, pl.ds(pl.multiple_of((i * groups + group) * piece, piece), piece)]
                for i in [sub + j for j in range(subs)]
            ],
            axis=1,
        )

    own_pair = (a % 4) // 2 * 2
    last_targets = targets_of(order[-1], 2 - own_pair, 2)

    @pl.loop(0, count // big)
    def _(t):
        start = pl.multiple_of(t * big, big)
        last_hot[pl.ds(start, big), :] = one_hot(rows_of((big, 2 * piece), start) == last_targets)

    for copy in parcels:
        copy.wait_recv()
    own = pl.multiple_of(g * piece, piece)
    terms = [lambda c: packets[pl.ds(own + c, LANES), :].astype(f32)]
    marked = [lambda line: packet_marks[g, line : line + 1, :]]
    for d in range(groups - 1):
        terms.append(lambda c, d=d: inbox[d, c : c + LANES, :].astype(f32))
        marked.append(lambda line, d=d: inbox_marks[d, line : line + 1, :])

    def piece_of(sub, group):
        return pl.ds(pl.multiple_of((group * 4 + sub % 4) * piece, piece), piece)

    base_three = pl.multiple_of((g * 4 + a % 4) * piece, piece)
    for c in range(0, piece, LANES):
        total, marks = 0.0, 0.0
        for term, marked_by in zip(terms, marked):
            got = spread(marked_by(c // LANES))
            marks = marks + got
            total = total + widened(got, features) * term(c)
        level = refined(total, widened(marks, features), coarse_ref[2])
        level_three[pl.ds(base_three + c, LANES), :] = level.astype(bf16)

    def relay(stage, leaves, comes, rows, peer):
        there = level_three.at[rows, :]
        return pltpu.make_async_remote_copy(
            src_ref=there,
            dst_ref=there,
            send_sem=spread_sems.at[0, stage, leaves],
            recv_sem=spread_sems.at[1, stage, comes],
            device_id=peer,
            device_id_type=pl.DeviceIdType.MESH,
        )

    def lift(group, sub, subs, last):
        width = subs * piece
        rows = pl.ds(pl.multiple_of((group * 4 + sub) * piece, piece), width)
        targets = None if last else targets_of(group, sub, subs)

        @pl.loop(0, count // big)
        def _(t):
            start = pl.multiple_of(t * big, big)
            here = pl.ds(start, big)
            if last:
                total = raised[here, :] + dot(last_hot[here, :], level_three[rows, :])
                present = fine_ref[here, 0:LANES].astype(f32)[:, 0:1] < LIMIT
                out_ref[here, :] = jnp.where(present, total, 0.0).astype(bf16)
            else:
                sel = one_hot(rows_of((big, width), start) == targets)
                raised[here, :] += dot(sel, level_three[rows, :])

    over_x, over_core, relayed = [], [], []

    def pass_on(group):
        over_x.append(relay(1, group, group, piece_of(a, group), {"sub": across}))
        over_x[-1].start()
        over_core.append(relay(2, group, group, piece_of(a, group), {"sub": core}))
        over_core[-1].start()

    def finish(k, last):
        group = order[k]
        over_x[k].wait_recv()
        relayed.append(relay(3, group, group, piece_of(across, group), {"sub": core}))
        relayed[k].start()
        over_core[k].wait_recv()
        if last:
            lift(group, own_pair, 2, False)
            relayed[k].wait_recv()
            lift(group, 2 - own_pair, 2, True)
        else:
            relayed[k].wait_recv()
            lift(group, 0, 4, False)

    mine_at = piece_of(a, g)
    pass_on(g)
    over_z = [relay(0, t, g, mine_at, {"grp": t}) for t in order[1:3]]
    for copy in over_z:
        copy.start()
    inner = g % 3 != 0
    mid, far = order[2:]

    def arrival(source):
        return relay(0, source, source, piece_of(a, source), {"grp": source})

    def hop(source):
        there = level_three.at[piece_of(a, source), :]
        return pltpu.make_async_remote_copy(
            src_ref=there,
            dst_ref=there,
            send_sem=spread_sems.at[0, 4, source],
            recv_sem=spread_sems.at[1, 0, source],
            device_id={"grp": near},
            device_id_type=pl.DeviceIdType.MESH,
        )

    arrival(near).wait_recv()
    pass_on(near)
    for k, source in ((0, mid), (1, far)):

        @pl.when(inner)
        def _():
            arrival(source).wait_recv()
            hop(source).start()

        finish(k, False)

        @pl.when(jnp.logical_not(inner))
        def _():
            arrival(source).wait_recv()

        pass_on(source)
    finish(2, False)
    finish(3, True)

    @pl.when(inner)
    def _():
        hop(mid).wait_send()
        hop(far).wait_send()

    for copy in sides + quads + quad_marks + twos + parcels + over_z + over_x + over_core + relayed:
        copy.wait_send()


def body(
    node_rows,
    owners,
    tile_src,
    neighbors,
    pool_pair,
    pool_quad,
    pool_top,
    edge_in,
    edge_bias,
    edge_out,
    node_in,
    node_bias,
    node_out,
    out_gain,
    coarse,
):
    groups = lax.axis_size("grp")
    owner_count = lax.axis_size("sub") * groups
    count, near_count = neighbors.shape[2:]
    nodes, features = node_rows.shape
    cap = count // owner_count
    half, quarter = count // 2, count // 4
    piece = quarter // groups
    tile = 256

    def shape(rows, dtype=bf16, width=features):
        return jax.ShapeDtypeStruct((rows, width), dtype)

    def room(like):
        return pltpu.VMEM(like.shape, like.dtype)

    pair = pool_pair.reshape(1, count)
    edge_row, node_row = edge_bias.reshape(1, features), node_bias.reshape(1, features)
    rows = pltpu.VMEM((count, features), bf16)
    sums = pltpu.VMEM((8, count), f32)
    square = pltpu.VMEM((features, features), bf16)
    slots = pl.pallas_call(
        functools.partial(slot_kernel, cap),
        out_shape=shape(1, jnp.int32, nodes),
        in_specs=[VM],
        out_specs=VM,
        compiler_params=pltpu.CompilerParams(vmem_limit_bytes=8 << 20),
        cost_estimate=pl.CostEstimate(
            flops=20 * 10**9, bytes_accessed=8 << 20, transcendentals=0
        ),
    )(owners.reshape(1, nodes))
    arrived, dst, src, lifted, near, to_two, to_three, pair_hot = pl.pallas_call(
        functools.partial(owner_kernel, groups, cap),
        out_shape=(
            shape(count),
            shape(count),
            shape(count),
            shape(count, f32),
            jax.ShapeDtypeStruct(neighbors.shape[2:], jnp.int32),
            shape(1, jnp.int32, count),
            shape(1, jnp.int32, count),
            shape(count, bf16, count),
        ),
        in_specs=[VM] + [HB] * 9,
        out_specs=(VM,) * 8,
        scratch_shapes=[
            room(node_rows),
            pltpu.VMEM((near_count, count), jnp.int32),
            room(pair),
            room(pool_quad),
            room(pool_top),
            room(edge_in),
            room(edge_row),
            square,
            room(node_row),
            sums,
            sums,
            rows,
            pltpu.SemaphoreType.DMA((9,)),
            pltpu.SemaphoreType.DMA((2, owner_count)),
        ],
        compiler_params=pltpu.CompilerParams(
            collective_id=1, has_side_effects=True, vmem_limit_bytes=24 << 20
        ),
    )(
        slots,
        node_rows,
        jnp.swapaxes(neighbors, 2, 3),
        pair,
        pool_quad,
        pool_top,
        edge_in,
        edge_row,
        node_in,
        node_row,
    )
    gathered = pltpu.VMEM((TPB * NBR * BLK, features), bf16)
    fine = pl.pallas_call(
        fine_kernel,
        out_shape=shape(count),
        in_specs=[SM] + [VM] * 5 + [HB] * 3 + [VM],
        out_specs=VM,
        scratch_shapes=[square] * 3
        + [
            rows,
            pltpu.VMEM((2, TPB * NBR * BLK, 2 * BLK), bf16),
            pltpu.VMEM((2, TPB, 2 * BLK, features), bf16),
            gathered,
            gathered,
            pltpu.SemaphoreType.DMA((3,)),
        ],
        compiler_params=pltpu.CompilerParams(vmem_limit_bytes=28 << 20),
        cost_estimate=pl.CostEstimate(
            flops=20 * 10**9, bytes_accessed=8 << 20, transcendentals=0
        ),
    )(
        jnp.swapaxes(tile_src, 2, 3),
        arrived,
        dst,
        src,
        lifted,
        near,
        edge_out,
        node_in,
        node_out,
        out_gain.reshape(1, features),
    )
    wide = pltpu.VMEM((count, features + LANES), bf16)
    pooled = pltpu.VMEM((half, features), bf16)
    marks = pltpu.VMEM((half // tile, MARKS, LANES), f32)
    return pl.pallas_call(
        functools.partial(tree_kernel, groups),
        out_shape=shape(count),
        in_specs=[VM] * 8,
        out_specs=VM,
        scratch_shapes=[
            rows,
            rows,
            rows,
            wide,
            pooled,
            pooled,
            marks,
            marks,
            wide,
            pltpu.VMEM((groups * piece, features), bf16),
            pltpu.VMEM((groups - 1, piece, features), bf16),
            pltpu.VMEM((groups, MARKS, LANES), f32),
            pltpu.VMEM((groups - 1, MARKS, LANES), f32),
            rows,
            pltpu.VMEM((count, features), f32),
            pltpu.VMEM((quarter, count), bf16),
            pltpu.VMEM((quarter, features + LANES), f32),
            pltpu.VMEM((count, 2 * piece), bf16),
            pltpu.SemaphoreType.DMA((2, count // 1024)),
            pltpu.SemaphoreType.DMA((2, half // tile)),
            pltpu.SemaphoreType.DMA((2, half // tile)),
            pltpu.SemaphoreType.DMA((2, half // tile)),
            pltpu.SemaphoreType.DMA((2, groups)),
            pltpu.SemaphoreType.DMA((2, groups)),
            pltpu.SemaphoreType.DMA((2, 5, groups)),
        ],
        compiler_params=pltpu.CompilerParams(
            collective_id=0, has_side_effects=True, vmem_limit_bytes=40 << 20
        ),
    )(fine, pair, pair_hot, pool_quad, pool_top, to_two, to_three, coarse)


def solution(mesh):
    in_specs = (
        P(("sub", "grp"), None),
        P(("sub", "grp")),
        P("sub", "grp", None, None),
        P("sub", "grp", None, None),
        P("sub", "grp", None),
        P(None, "grp", None),
        P(None, "grp", None),
        P(),
        P(),
        P(),
        P(),
        P(),
        P(),
        P(),
        P(),
    )
    out_specs = P(("sub", "grp"), None)
    return jax.shard_map(body, mesh=mesh, in_specs=in_specs, out_specs=out_specs, check_vma=False)
```

```python
import functools

import jax
import jax.numpy as jnp
from jax import lax
from jax.experimental import pallas as pl
from jax.experimental.pallas import tpu as pltpu
from jax.sharding import PartitionSpec as P

BLK = 128
TPB = 2
NBR = 8
LANES = 128
PAD = 16
MARKS = 8
EMPTY = 16384.0
LIMIT = 8192.0
AWAY = -8192.0
epsilon = 1e-05
f32 = jnp.float32
bf16 = jnp.bfloat16

VM = pl.BlockSpec(memory_space=pltpu.VMEM)
SM = pl.BlockSpec(memory_space=pltpu.SMEM)
HB = pl.BlockSpec(memory_space=pltpu.HBM)


def rows_of(shape, start=0):
    return lax.broadcasted_iota(jnp.int32, shape, 0) + start


def lanes_of(shape, start=0):
    return lax.broadcasted_iota(jnp.int32, shape, 1) + start


def one_hot(mask):
    return jnp.where(mask, 1.0, 0.0).astype(bf16)


def spread(row):
    return jnp.broadcast_to(row, (LANES, LANES)).T


def dot(a, b):
    return jnp.dot(a, b, preferred_element_type=f32)


def half_silu(h):
    return h + h * jnp.tanh(h)


def picker(perm_ref, first, count, start, width):
    tiles = []
    for c in range(0, count, LANES):
        column = spread(perm_ref[:, pl.ds(pl.multiple_of(first + c, LANES), LANES)])
        wide = jnp.concatenate([column] * (width // LANES), axis=1)
        tiles.append(one_hot(wide == lanes_of((LANES, width), start)))
    return jnp.concatenate(tiles, axis=0)


def refined(total, count, weight):
    mean_rows = total * (1.0 / jnp.maximum(count, 1.0))
    lifted = dot(mean_rows.astype(bf16), weight)
    return mean_rows + half_silu(lifted * 0.5)


def widened(column, features):
    return jnp.concatenate([column] * (features // LANES), axis=1)


def put_marks(out_ref, at, columns):
    lines = [col.T[0:1, :] for col in columns]
    lines.append(jnp.zeros((MARKS - len(lines), LANES), f32))
    out_ref[at] = jnp.concatenate(lines, axis=0)


def slot_kernel(cap, owners_ref, slots_ref):
    nodes = owners_ref.shape[1]
    owner_row = owners_ref[...]
    position = jnp.zeros((1, nodes), f32)
    for c in range(0, nodes, LANES):
        column = spread(owners_ref[:, c : c + LANES])
        wide = jnp.concatenate([column] * (nodes // LANES), axis=1)
        shape = (LANES, nodes)
        earlier = (wide == owner_row) & (rows_of(shape, c) < lanes_of(shape))
        position += jnp.sum(jnp.where(earlier, 1.0, 0.0), axis=0, keepdims=True)
    slots_ref[...] = owner_row * cap + position.astype(jnp.int32)


def owner_kernel(
    groups,
    cap,
    slots_ref,
    node_rows_hbm,
    near_hbm,
    pair_hbm,
    quad_hbm,
    top_hbm,
    edge_in_hbm,
    edge_bias_hbm,
    node_in_hbm,
    node_bias_hbm,
    arrived,
    dst,
    src,
    raised,
    near_ref,
    two_ref,
    three_ref,
    pair_hot,
    nodes_ref,
    near_rows,
    pair_ref,
    quads_ref,
    tops_ref,
    edge_in_ref,
    edge_bias_ref,
    node_in_ref,
    node_bias_ref,
    parts,
    sums,
    placed,
    load_sems,
    place_sems,
):
    count, features = arrived.shape
    nodes = nodes_ref.shape[0]
    tile = 256
    a, g = lax.axis_index("sub"), lax.axis_index("grp")
    me = a * groups + g
    owners = count // cap
    per_tile = tile // cap
    tiles = count // tile

    def mesh_place(owner):
        return {"sub": owner // groups, "grp": owner % groups}

    barrier = pltpu.get_barrier_semaphore()

    @pl.loop(0, owners)
    def _(owner):
        @pl.when(owner != me)
        def _():
            pl.semaphore_signal(
                barrier,
                inc=1,
                device_id=mesh_place(owner),
                device_id_type=pl.DeviceIdType.MESH,
            )

    loads = []
    for source, target in (
        (node_rows_hbm, nodes_ref),
        (edge_in_hbm, edge_in_ref),
        (edge_bias_hbm, edge_bias_ref),
        (node_in_hbm.at[0], node_in_ref),
        (node_bias_hbm, node_bias_ref),
        (pair_hbm, pair_ref),
        (quad_hbm, quads_ref),
        (top_hbm, tops_ref),
        (near_hbm.at[0, 0], near_rows),
    ):
        copy = pltpu.make_async_copy(source, target, load_sems.at[len(loads)])
        copy.start()
        loads.append(copy)

    slot_of = slots_ref[...]
    loads[0].wait()
    pl.semaphore_wait(barrier, owners - 1)

    def of_owner(owner):
        return pl.ds(pl.multiple_of(owner * cap, PAD), cap)

    def delivery(owner, sender):
        return pltpu.make_async_remote_copy(
            src_ref=placed.at[of_owner(owner), :],
            dst_ref=arrived.at[of_owner(sender), :],
            send_sem=place_sems.at[0, owner],
            recv_sem=place_sems.at[1, sender],
            device_id=mesh_place(owner),
            device_id_type=pl.DeviceIdType.MESH,
        )

    @pl.loop(0, tiles)
    def _(step):
        t = lax.rem(a + step, tiles)
        start = pl.multiple_of(t * tile, tile)
        weight = jnp.where(rows_of((tile, nodes), start) == slot_of, 1.0, 0.0)
        filled = jnp.max(weight, axis=1, keepdims=True)
        rows = dot(weight.astype(bf16), nodes_ref[...])
        placed[pl.ds(start, tile), :] = jnp.where(filled > 0.5, rows, EMPTY).astype(bf16)

        @pl.loop(0, per_tile)
        def _(k):
            owner = t * per_tile + k

            @pl.when(owner != me)
            def _():
                delivery(owner, me).start()

    arrived[of_owner(me), :] = placed[of_owner(me), :]

    for copy in loads[5:8]:
        copy.wait()
    quad_ref, top_ref = quads_ref.at[a // 2], tops_ref.at[a // 4]

    def compose(outer, inner_row, target_ref):
        which = rows_of((8, count))
        high = (outer >> 7).astype(f32)
        low = (outer & 127).astype(f32)
        parts[...] = jnp.where(which == 0, high, jnp.where(which == 1, low, 0.0))
        sums[...] = jnp.zeros_like(sums)

        @pl.loop(0, tiles)
        def _(t):
            start = pl.multiple_of(t * tile, tile)
            sel = one_hot(rows_of((tile, count), start) == inner_row)
            sums[...] += dot(parts[:, pl.ds(start, tile)].astype(bf16), sel)

        total = sums[...]
        target_ref[...] = (total[0:1] * 128.0 + total[1:2]).astype(jnp.int32)

    compose(pair_ref[...], quad_ref[...], two_ref)
    compose(two_ref[...], top_ref[...], three_ref)
    for copy in loads[1:5] + loads[8:]:
        copy.wait()
    near_count = near_ref.shape[1]

    @pl.loop(0, tiles)
    def _(t):
        start = pl.multiple_of(t * tile, tile)
        pair_hot[pl.ds(start, tile), :] = picker(pair_ref, start, tile, 0, count)

    @pl.loop(0, count // LANES)
    def _(t):
        here = pl.ds(pl.multiple_of(t * LANES, LANES), LANES)
        turned = jnp.concatenate([near_rows[:, here]] * (LANES // near_count), axis=0).T
        near_ref[here, :] = turned[:, 0:near_count]

    @pl.loop(0, tiles)
    def _(step):
        t = lax.rem(a - step + tiles * owners, tiles)

        @pl.loop(0, per_tile)
        def _(k):
            sender = t * per_tile + k

            @pl.when(sender != me)
            def _():
                delivery(me, sender).wait_recv()

        here = pl.ds(pl.multiple_of(t * tile, tile), tile)
        raw = arrived[here, :].astype(f32)
        present = raw[:, 0:1] < LIMIT
        rows = jnp.where(present, raw, 0.0).astype(bf16)
        to_dst = (dot(rows, edge_in_ref[0]) + edge_bias_ref[...]) * 0.5
        dst[here, :] = to_dst.astype(bf16)
        from_src = dot(rows, edge_in_ref[1]) * 0.5
        src[here, :] = jnp.where(present, from_src, AWAY).astype(bf16)
        raised[here, :] = dot(rows, node_in_ref[...]) + node_bias_ref[...]

    @pl.loop(0, owners)
    def _(owner):
        @pl.when(owner != me)
        def _():
            delivery(owner, me).wait_send()


def fine_kernel(
    tile_src_ref,
    arrived,
    dst,
    src,
    raised,
    near_ref,
    edge_out_hbm,
    node_in_hbm,
    node_out_hbm,
    gain_ref,
    fine_ref,
    edge_out_ref,
    node_in_ref,
    node_out_ref,
    agg,
    sels,
    weights,
    near_a,
    near_b,
    load_sems,
):
    count, features = fine_ref.shape
    tile = 256
    tiles = count // tile
    loads = []
    for source, target in (
        (edge_out_hbm, edge_out_ref),
        (node_in_hbm.at[1], node_in_ref),
        (node_out_hbm, node_out_ref),
    ):
        copy = pltpu.make_async_copy(source, target, load_sems.at[len(loads)])
        copy.start()
        loads.append(copy)

    many_near = 4
    pieces_near = TPB * NBR // many_near
    group = 32
    eye = one_hot(rows_of((BLK, BLK)) == lanes_of((BLK, BLK)))
    for p in range(2):
        for i in range(TPB * NBR):
            sels[p, i * BLK : (i + 1) * BLK, BLK : 2 * BLK] = eye

    def gather(b, p, near, i):
        start = pl.multiple_of(b * BLK, BLK)
        j = i * many_near // NBR
        if i * many_near % NBR == 0:
            first = pl.multiple_of(tile_src_ref[0, 0, j, b] * BLK, BLK)
            weights[p, j, 0:BLK, :] = src[pl.ds(first, BLK), :]
            weights[p, j, BLK : 2 * BLK, :] = dst[pl.ds(start, BLK), :]
        which = near_ref[pl.ds(start, BLK), :]
        for k in range(i * many_near, (i + 1) * many_near):
            mask = which[:, k : k + 1] == lanes_of((BLK, BLK))
            sels[p, k * BLK : (k + 1) * BLK, 0:BLK] = one_hot(mask)
        rows = slice(i * many_near * BLK, (i + 1) * many_near * BLK)
        near[rows, :] = dot(sels[p, rows, :], weights[p, j]).astype(bf16)

    def settle(b, near, r):
        total = jnp.zeros((group, features), f32)
        for k in range(0, TPB * NBR, 4):
            terms = [
                half_silu(near[at * BLK + r : at * BLK + r + group, :]) for at in range(k, k + 4)
            ]
            total += ((terms[0] + terms[1]) + (terms[2] + terms[3])).astype(f32)
        agg[pl.ds(pl.multiple_of(b * BLK, BLK) + r, group), :] = total.astype(bf16)

    def both(ahead, p, near_next, b, near):
        sums = BLK // group
        for i in range(max(pieces_near, sums)):
            if i * pieces_near % max(pieces_near, sums) == 0:
                gather(ahead, p, near_next, i * pieces_near // max(pieces_near, sums))
            if i * sums % max(pieces_near, sums) == 0:
                settle(b, near, i * sums // max(pieces_near, sums) * group)

    for i in range(pieces_near):
        gather(0, 0, near_a, i)
    blocks = count // BLK

    @pl.loop(0, blocks // 2)
    def _(h):
        b = 2 * h
        both(b + 1, 1, near_b, b, near_a)
        both(lax.rem(b + 2, blocks), 0, near_a, b + 1, near_b)

    for copy in loads:
        copy.wait()

    many = 1024

    @pl.loop(0, count // many)
    def _(t):
        here = pl.ds(pl.multiple_of(t * many, many), many)
        message = dot(agg[here, :], edge_out_ref[...]).astype(bf16)
        lifted = raised[here, :] + dot(message, node_in_ref[...])
        hidden = half_silu(lifted * 0.5).astype(bf16)
        delta = dot(hidden, node_out_ref[...])
        scale = lax.rsqrt(jnp.mean(delta * delta, axis=-1, keepdims=True) + epsilon)
        raw = arrived[here, :].astype(f32)
        fine = raw + gain_ref[...] * (delta * scale)
        fine_ref[here, :] = jnp.where(raw[:, 0:1] < LIMIT, fine, EMPTY).astype(bf16)


def tree_kernel(
    groups,
    fine_ref,
    pair_ref,
    pair_hot,
    quads_ref,
    tops_ref,
    two_ref,
    three_ref,
    coarse_ref,
    out_ref,
    side,
    partner,
    level_one,
    wide_one,
    mine,
    theirs,
    my_marks,
    their_marks,
    wide_two,
    packets,
    inbox,
    packet_marks,
    inbox_marks,
    level_three,
    raised,
    top_hot,
    picked,
    last_hot,
    side_sems,
    quad_sems,
    quad_mark_sems,
    two_sems,
    group_sems,
    group_mark_sems,
    spread_sems,
):
    count, features = fine_ref.shape
    half, quarter = count // 2, count // 4
    piece = quarter // groups
    tile, big = 256, 512
    a, g = lax.axis_index("sub"), lax.axis_index("grp")
    quad_ref, top_ref = quads_ref.at[a // 2], tops_ref.at[a // 4]
    core = a + 1 - 2 * (a % 2)
    across = a + 2 - 4 * ((a // 2) % 2)
    others = [lax.rem(g + d, groups) for d in range(1, groups)]
    peers = [{"grp": t} for t in others] + [{"sub": across}, {"sub": core}]
    barrier = pltpu.get_barrier_semaphore()
    for peer in peers:
        pl.semaphore_signal(barrier, inc=1, device_id=peer, device_id_type=pl.DeviceIdType.MESH)

    def send(sems, at, source, target, peer):
        copy = pltpu.make_async_remote_copy(
            src_ref=source,
            dst_ref=target,
            send_sem=sems.at[(0, *at)],
            recv_sem=sems.at[(1, *at)],
            device_id=peer,
            device_id_type=pl.DeviceIdType.MESH,
        )
        copy.start()
        return copy

    cuts = (0, half, half + quarter, count)
    sides = []
    for t, (first, end) in enumerate(zip(cuts[:-1], cuts[1:])):
        here = pl.ds(first, end - first)
        side[here, :] = dot(pair_hot[here, :], fine_ref[...]).astype(bf16)
        if t == 0:
            pl.semaphore_wait(barrier, len(peers))
        sides.append(send(side_sems, (t,), side.at[here, :], partner.at[here, :], {"sub": core}))
    for t, (first, end) in enumerate(zip(cuts[:-1], cuts[1:])):
        sides[t].wait_recv()
        for start in range(first, end, big):
            here = pl.ds(start, big)
            x = side[here, :].astype(f32)
            y = partner[here, :].astype(f32)
            in_x = x[:, 0:1] < LIMIT
            in_y = y[:, 0:1] < LIMIT
            total = jnp.where(in_x, x, 0.0) + jnp.where(in_y, y, 0.0)
            marks = jnp.where(in_x, 1.0, 0.0) + jnp.where(in_y, 1.0, 0.0)
            level = refined(total, marks, coarse_ref[0]).astype(bf16)
            level_one[here, :] = level
            wide_one[here, 0:features] = level
            wide_one[here, features : features + LANES] = jnp.broadcast_to(
                marks, (big, LANES)
            ).astype(bf16)

    quads, quad_marks = [], []
    for t in range(half // tile):
        sel = picker(quad_ref, (a % 2) * half + t * tile, tile, 0, count)
        got = dot(sel, wide_one[...])
        columns = [got[c : c + LANES, features : features + LANES] for c in range(0, tile, LANES)]
        put_marks(my_marks, t, columns)
        quad_marks.append(
            send(quad_mark_sems, (t,), my_marks.at[t], their_marks.at[t], {"sub": across})
        )
        here = pl.ds(t * tile, tile)
        mine[here, :] = got[:, 0:features].astype(bf16)
        quads.append(send(quad_sems, (t,), mine.at[here, :], theirs.at[here, :], {"sub": across}))

    @pl.loop(0, count // big)
    def _(t):
        start = pl.multiple_of(t * big, big)
        here = pl.ds(start, big)
        sel = one_hot(rows_of((big, count), start) == pair_ref[...])
        raised[here, :] = fine_ref[here, :].astype(f32) + dot(sel, level_one[...])

    top_hot[...] = picker(top_ref, (a % 4) * quarter, quarter, 0, count)
    base = pl.multiple_of((a % 2) * half, half)
    twos = []
    for t in range(half // tile):
        quads[t].wait_recv()
        quad_marks[t].wait_recv()
        for c in range(0, tile, LANES):
            line = c // LANES
            x = spread(my_marks[t, line : line + 1, :])
            y = spread(their_marks[t, line : line + 1, :])
            at = t * tile + c
            total = widened(x, features) * mine[at : at + LANES, :].astype(f32) + widened(
                y, features
            ) * theirs[at : at + LANES, :].astype(f32)
            level = refined(total, widened(x + y, features), coarse_ref[1])
            there = pl.ds(base + t * tile + c, LANES)
            wide_two[there, 0:features] = level.astype(bf16)
            wide_two[there, features : features + LANES] = (x + y).astype(bf16)
        there = wide_two.at[pl.ds(base + t * tile, tile), :]
        twos.append(send(two_sems, (t,), there, there, {"sub": core}))
        mine_here = pl.ds(pl.multiple_of(base + t * tile, tile), tile)
        part = dot(top_hot[:, mine_here], wide_two[mine_here, :])
        twos[t].wait_recv()
        their_here = pl.ds(pl.multiple_of(half - base + t * tile, tile), tile)
        part += dot(top_hot[:, their_here], wide_two[their_here, :])
        if t == 0:
            picked[...] = part
        else:
            picked[...] += part

    got = picked[...]
    for t in range(groups):
        at = t * piece
        packets[at : at + piece, :] = got[at : at + piece, 0:features].astype(bf16)
        columns = [
            got[at + c : at + c + LANES, features : features + LANES]
            for c in range(0, piece, LANES)
        ]
        put_marks(packet_marks, t, columns)
    parcels = []
    for d, t in enumerate(others):
        here = pl.ds(pl.multiple_of(t * piece, piece), piece)
        peer = {"grp": t}
        parcels.append(
            send(group_mark_sems, (d,), packet_marks.at[t], inbox_marks.at[d], peer)
        )
        parcels.append(send(group_sems, (d,), packets.at[here, :], inbox.at[d], peer))

    @pl.loop(0, count // big)
    def _(t):
        start = pl.multiple_of(t * big, big)
        here = pl.ds(start, big)
        sel = one_hot(rows_of((big, count), start) == two_ref[...])
        raised[here, :] += dot(sel, wide_two[:, 0:features])

    near = g + 1 - 2 * (g % 2)
    order = [g, near, 2 - g // 2, 3 - 3 * (g // 2)]

    def targets_of(group, sub, subs):
        return jnp.concatenate(
            [
                three_ref[:, pl.ds(pl.multiple_of((i * groups + group) * piece, piece), piece)]
                for i in [sub + j for j in range(subs)]
            ],
            axis=1,
        )

    own_pair = (a % 4) // 2 * 2
    last_targets = targets_of(order[-1], 2 - own_pair, 2)

    @pl.loop(0, count // big)
    def _(t):
        start = pl.multiple_of(t * big, big)
        last_hot[pl.ds(start, big), :] = one_hot(rows_of((big, 2 * piece), start) == last_targets)

    for copy in parcels:
        copy.wait_recv()
    own = pl.multiple_of(g * piece, piece)
    terms = [lambda c: packets[pl.ds(own + c, LANES), :].astype(f32)]
    marked = [lambda line: packet_marks[g, line : line + 1, :]]
    for d in range(groups - 1):
        terms.append(lambda c, d=d: inbox[d, c : c + LANES, :].astype(f32))
        marked.append(lambda line, d=d: inbox_marks[d, line : line + 1, :])

    def piece_of(sub, group):
        return pl.ds(pl.multiple_of((group * 4 + sub % 4) * piece, piece), piece)

    base_three = pl.multiple_of((g * 4 + a % 4) * piece, piece)
    for c in range(0, piece, LANES):
        total, marks = 0.0, 0.0
        for term, marked_by in zip(terms, marked):
            got = spread(marked_by(c // LANES))
            marks = marks + got
            total = total + widened(got, features) * term(c)
        level = refined(total, widened(marks, features), coarse_ref[2])
        level_three[pl.ds(base_three + c, LANES), :] = level.astype(bf16)

    def relay(stage, leaves, comes, rows, peer):
        there = level_three.at[rows, :]
        return pltpu.make_async_remote_copy(
            src_ref=there,
            dst_ref=there,
            send_sem=spread_sems.at[0, stage, leaves],
            recv_sem=spread_sems.at[1, stage, comes],
            device_id=peer,
            device_id_type=pl.DeviceIdType.MESH,
        )

    def lift(group, sub, subs, last):
        width = subs * piece
        rows = pl.ds(pl.multiple_of((group * 4 + sub) * piece, piece), width)
        targets = None if last else targets_of(group, sub, subs)

        @pl.loop(0, count // big)
        def _(t):
            start = pl.multiple_of(t * big, big)
            here = pl.ds(start, big)
            if last:
                total = raised[here, :] + dot(last_hot[here, :], level_three[rows, :])
                present = fine_ref[here, 0:LANES].astype(f32)[:, 0:1] < LIMIT
                out_ref[here, :] = jnp.where(present, total, 0.0).astype(bf16)
            else:
                sel = one_hot(rows_of((big, width), start) == targets)
                raised[here, :] += dot(sel, level_three[rows, :])

    over_x, over_core, relayed = [], [], []

    def pass_on(group):
        over_x.append(relay(1, group, group, piece_of(a, group), {"sub": across}))
        over_x[-1].start()
        over_core.append(relay(2, group, group, piece_of(a, group), {"sub": core}))
        over_core[-1].start()

    def finish(k, last):
        group = order[k]
        over_x[k].wait_recv()
        relayed.append(relay(3, group, group, piece_of(across, group), {"sub": core}))
        relayed[k].start()
        over_core[k].wait_recv()
        if last:
            lift(group, own_pair, 2, False)
            relayed[k].wait_recv()
            lift(group, 2 - own_pair, 2, True)
        else:
            relayed[k].wait_recv()
            lift(group, 0, 4, False)

    mine_at = piece_of(a, g)
    pass_on(g)
    over_z = [relay(0, t, g, mine_at, {"grp": t}) for t in order[1:3]]
    for copy in over_z:
        copy.start()
    inner = g % 3 != 0
    mid, far = order[2:]

    def arrival(source):
        return relay(0, source, source, piece_of(a, source), {"grp": source})

    def hop(source):
        there = level_three.at[piece_of(a, source), :]
        return pltpu.make_async_remote_copy(
            src_ref=there,
            dst_ref=there,
            send_sem=spread_sems.at[0, 4, source],
            recv_sem=spread_sems.at[1, 0, source],
            device_id={"grp": near},
            device_id_type=pl.DeviceIdType.MESH,
        )

    arrival(near).wait_recv()
    pass_on(near)
    for k, source in ((0, mid), (1, far)):

        @pl.when(inner)
        def _():
            arrival(source).wait_recv()
            hop(source).start()

        finish(k, False)

        @pl.when(jnp.logical_not(inner))
        def _():
            arrival(source).wait_recv()

        pass_on(source)
    finish(2, False)
    finish(3, True)

    @pl.when(inner)
    def _():
        hop(mid).wait_send()
        hop(far).wait_send()

    for copy in sides + quads + quad_marks + twos + parcels + over_z + over_x + over_core + relayed:
        copy.wait_send()


def body(
    node_rows,
    owners,
    tile_src,
    neighbors,
    pool_pair,
    pool_quad,
    pool_top,
    edge_in,
    edge_bias,
    edge_out,
    node_in,
    node_bias,
    node_out,
    out_gain,
    coarse,
):
    groups = lax.axis_size("grp")
    owner_count = lax.axis_size("sub") * groups
    count, near_count = neighbors.shape[2:]
    nodes, features = node_rows.shape
    cap = count // owner_count
    half, quarter = count // 2, count // 4
    piece = quarter // groups
    tile = 256

    def shape(rows, dtype=bf16, width=features):
        return jax.ShapeDtypeStruct((rows, width), dtype)

    def room(like):
        return pltpu.VMEM(like.shape, like.dtype)

    pair = pool_pair.reshape(1, count)
    edge_row, node_row = edge_bias.reshape(1, features), node_bias.reshape(1, features)
    rows = pltpu.VMEM((count, features), bf16)
    sums = pltpu.VMEM((8, count), f32)
    square = pltpu.VMEM((features, features), bf16)
    slots = pl.pallas_call(
        functools.partial(slot_kernel, cap),
        out_shape=shape(1, jnp.int32, nodes),
        in_specs=[VM],
        out_specs=VM,
        compiler_params=pltpu.CompilerParams(vmem_limit_bytes=8 << 20),
        cost_estimate=pl.CostEstimate(
            flops=20 * 10**9, bytes_accessed=8 << 20, transcendentals=0
        ),
    )(owners.reshape(1, nodes))
    arrived, dst, src, lifted, near, to_two, to_three, pair_hot = pl.pallas_call(
        functools.partial(owner_kernel, groups, cap),
        out_shape=(
            shape(count),
            shape(count),
            shape(count),
            shape(count, f32),
            jax.ShapeDtypeStruct(neighbors.shape[2:], jnp.int32),
            shape(1, jnp.int32, count),
            shape(1, jnp.int32, count),
            shape(count, bf16, count),
        ),
        in_specs=[VM] + [HB] * 9,
        out_specs=(VM,) * 8,
        scratch_shapes=[
            room(node_rows),
            pltpu.VMEM((near_count, count), jnp.int32),
            room(pair),
            room(pool_quad),
            room(pool_top),
            room(edge_in),
            room(edge_row),
            square,
            room(node_row),
            sums,
            sums,
            rows,
            pltpu.SemaphoreType.DMA((9,)),
            pltpu.SemaphoreType.DMA((2, owner_count)),
        ],
        compiler_params=pltpu.CompilerParams(
            collective_id=1, has_side_effects=True, vmem_limit_bytes=24 << 20
        ),
    )(
        slots,
        node_rows,
        jnp.swapaxes(neighbors, 2, 3),
        pair,
        pool_quad,
        pool_top,
        edge_in,
        edge_row,
        node_in,
        node_row,
    )
    gathered = pltpu.VMEM((TPB * NBR * BLK, features), bf16)
    fine = pl.pallas_call(
        fine_kernel,
        out_shape=shape(count),
        in_specs=[SM] + [VM] * 5 + [HB] * 3 + [VM],
        out_specs=VM,
        scratch_shapes=[square] * 3
        + [
            rows,
            pltpu.VMEM((2, TPB * NBR * BLK, 2 * BLK), bf16),
            pltpu.VMEM((2, TPB, 2 * BLK, features), bf16),
            gathered,
            gathered,
            pltpu.SemaphoreType.DMA((3,)),
        ],
        compiler_params=pltpu.CompilerParams(vmem_limit_bytes=28 << 20),
        cost_estimate=pl.CostEstimate(
            flops=20 * 10**9, bytes_accessed=8 << 20, transcendentals=0
        ),
    )(
        jnp.swapaxes(tile_src, 2, 3),
        arrived,
        dst,
        src,
        lifted,
        near,
        edge_out,
        node_in,
        node_out,
        out_gain.reshape(1, features),
    )
    wide = pltpu.VMEM((count, features + LANES), bf16)
    pooled = pltpu.VMEM((half, features), bf16)
    marks = pltpu.VMEM((half // tile, MARKS, LANES), f32)
    return pl.pallas_call(
        functools.partial(tree_kernel, groups),
        out_shape=shape(count),
        in_specs=[VM] * 8,
        out_specs=VM,
        scratch_shapes=[
            rows,
            rows,
            rows,
            wide,
            pooled,
            pooled,
            marks,
            marks,
            wide,
            pltpu.VMEM((groups * piece, features), bf16),
            pltpu.VMEM((groups - 1, piece, features), bf16),
            pltpu.VMEM((groups, MARKS, LANES), f32),
            pltpu.VMEM((groups - 1, MARKS, LANES), f32),
            rows,
            pltpu.VMEM((count, features), f32),
            pltpu.VMEM((quarter, count), bf16),
            pltpu.VMEM((quarter, features + LANES), f32),
            pltpu.VMEM((count, 2 * piece), bf16),
            pltpu.SemaphoreType.DMA((2, 3)),
            pltpu.SemaphoreType.DMA((2, half // tile)),
            pltpu.SemaphoreType.DMA((2, half // tile)),
            pltpu.SemaphoreType.DMA((2, half // tile)),
            pltpu.SemaphoreType.DMA((2, groups)),
            pltpu.SemaphoreType.DMA((2, groups)),
            pltpu.SemaphoreType.DMA((2, 5, groups)),
        ],
        compiler_params=pltpu.CompilerParams(
            collective_id=0, has_side_effects=True, vmem_limit_bytes=40 << 20
        ),
    )(fine, pair, pair_hot, pool_quad, pool_top, to_two, to_three, coarse)


def solution(mesh):
    in_specs = (
        P(("sub", "grp"), None),
        P(("sub", "grp")),
        P("sub", "grp", None, None),
        P("sub", "grp", None, None),
        P("sub", "grp", None),
        P(None, "grp", None),
        P(None, "grp", None),
        P(),
        P(),
        P(),
        P(),
        P(),
        P(),
        P(),
        P(),
    )
    out_specs = P(("sub", "grp"), None)
    return jax.shard_map(body, mesh=mesh, in_specs=in_specs, out_specs=out_specs, check_vma=False)
```
